32 devices in a mesh: row: 4 (over z), col: 8 (over y, x, core).
Axes of the slice: x: 2, y: 2, z: 4, core: 2. Of those that a mesh axis runs over, the one named last changes fastest.
Arguments:
- examples: bfloat16 [65536, 1024], P(('row', 'col')), may hold values from -20 to 20
- residuals: float32 [65536, 256], P(('row', 'col')), may hold values from -6 to 6
- coefficients: float32 [65536, 256], P(('row', 'col')), may hold values from -0.8 to 0.8
- block_index: int32 [1], replicated, may hold values from 0 to 63
Outputs:
- new_residuals: float32 [65536, 256], P(('row', 'col'))
- new_coefficients: float32 [65536, 256], P(('row', 'col'))
The draws below stay inside these ranges and needn't reach their ends.
All inputs are finite; a program needn't handle non-finite values.
Results may differ from the reference program's by a relative error of at most 0.00035.
Values may be sent and summed in bfloat16 or wider, within the bound.
No kernel may reach another device: no remote copies, remote signals or barrier semaphores. Data moves between devices by JAX's collectives and lax.ppermute only.
A program may use at most 128 MiB of HBM per device.

```python
import math
import jax
import jax.numpy as jnp
from jax import lax

FEATURES = 1024
OUTPUTS = 256
BLOCK = 1024
EX_DEV = 2048
EXAMPLES = 65536


def draw_examples(key, part):
    latent_count = 6
    key_latent = jax.random.fold_in(key, 11)
    key_mixing = jax.random.fold_in(key, 12)
    key_noise = jax.random.fold_in(key, 13)
    mixing = jax.random.normal(key_mixing, (latent_count, FEATURES), jnp.float32) / math.sqrt(latent_count)
    spread = math.sqrt(2.0 * latent_count)
    latent = jax.random.normal(key_latent, (EXAMPLES, latent_count), jnp.float32)
    noise = 0.5 * jax.random.normal(key_noise, (EXAMPLES, FEATURES), jnp.float32)
    values = spread * jnp.dot(latent, mixing, precision=lax.Precision.HIGHEST) + noise
    return jnp.clip(values, -20.0, 20.0).astype(jnp.bfloat16)


def block_scale(stream_key, shape, split, least, high):
    factor_of, own = 1.0, jax.random.fold_in(stream_key, 6)
    for axis_at, blocks in split:
        heights = jnp.exp(jax.random.uniform(jax.random.fold_in(own, axis_at), (blocks,), jnp.float32, least / len(split), high / len(split)))
        factor_of = factor_of * jnp.repeat(heights, shape[axis_at] // blocks).reshape([-1 if axis == axis_at else 1 for axis in range(len(shape))])
    return factor_of


def normal_values(stream_key, extent, scale, limit, cuts=(), kind=jnp.bfloat16):
    result = jax.random.normal(stream_key, extent, jnp.float32) * scale
    if len(cuts) > 0:
        result = block_scale(stream_key, extent, cuts, -0.22, 0.18) * result
    return jnp.clip(result, min=-limit, max=limit).astype(kind)


def setup_inputs(seed: int = 0) -> dict:
    key_of = jax.random.split(jax.random.key(seed), 5)
    return {
        "examples": draw_examples(jax.random.fold_in(key_of[4], 71), 0),
        "residuals": normal_values(key_of[1], (EXAMPLES, OUTPUTS), 1.0, 6.0, ((0, 32),), jnp.float32),
        "coefficients": normal_values(key_of[2], (EXAMPLES, OUTPUTS), 0.1, 0.8, ((0, 32),), jnp.float32),
        "block_index": jax.random.randint(key_of[3], (1,), 0, EXAMPLES // BLOCK).astype(jnp.int32),
    }


ridge = 0.001
width_factor = 0.5

def reference(examples, residuals, coefficients, block_index):
    chosen = block_index[0].astype(jnp.int32)
    start = (chosen * BLOCK).astype(jnp.int32)
    block_rows = lax.dynamic_slice_in_dim(examples, start, BLOCK, 0)
    block_coef = lax.dynamic_slice_in_dim(coefficients, start, BLOCK, 0)
    sq_block = jnp.sum(jnp.square(block_rows.astype(jnp.float32)), axis=1)
    shards = EXAMPLES // EX_DEV
    grouped = examples.reshape(shards, EX_DEV, FEATURES)
    grouped_res = residuals.reshape(shards, EX_DEV, OUTPUTS)

    def one_shard(carry, pair):
        rows, res = pair
        sq_rows = jnp.sum(jnp.square(rows.astype(jnp.float32)), axis=1)
        inner = jnp.dot(rows.astype(jnp.float32), block_rows.T.astype(jnp.float32), preferred_element_type=jnp.float32)
        kernel = jnp.exp(-width_factor * (sq_rows[:, None] + sq_block[None, :] - 2.0 * inner) / FEATURES).astype(jnp.bfloat16)
        residual_low = res.astype(jnp.bfloat16)
        grad_part = jnp.dot(kernel.T.astype(jnp.float32), residual_low.astype(jnp.float32), preferred_element_type=jnp.float32)
        gram_part = jnp.dot(kernel.T.astype(jnp.float32), kernel.astype(jnp.float32), preferred_element_type=jnp.float32)
        return ((carry[0] + grad_part, carry[1] + gram_part), kernel)
    init = (jnp.zeros((BLOCK, OUTPUTS), jnp.float32), jnp.zeros((BLOCK, BLOCK), jnp.float32))
    (grad, gram), kernels = lax.scan(one_shard, init, (grouped, grouped_res))
    grad = grad - EXAMPLES * ridge * block_coef
    system = gram / EXAMPLES + ridge * jnp.eye(BLOCK, dtype=jnp.float32)
    factor = jnp.linalg.cholesky(system)
    update = jax.scipy.linalg.cho_solve((factor, True), grad / EXAMPLES)
    update_low = update.astype(jnp.bfloat16)

    def apply_shard(kernel):
        return jnp.dot(kernel.astype(jnp.float32), update_low.astype(jnp.float32), preferred_element_type=jnp.float32)
    change = lax.map(apply_shard, kernels).reshape(EXAMPLES, OUTPUTS)
    new_residuals = residuals - change
    new_coefficients = lax.dynamic_update_slice_in_dim(coefficients, block_coef + update, start, 0)
    return (new_residuals, new_coefficients)
```

```python
import functools

import jax
import jax.numpy as jnp
from jax import lax
from jax.experimental import pallas as pl
from jax.experimental.pallas import tpu as pltpu
from jax.sharding import PartitionSpec as P

BLOCK = 1024
TILE = 128
SUB = 8
AXES = ("row", "col")

ridge = 0.001
width_factor = 0.5
HIGHEST = lax.Precision.HIGHEST
f32 = jnp.float32
bf16 = jnp.bfloat16


def swap(value, bit):
    axis, mask = bit
    size = lax.axis_size(axis)
    return lax.ppermute(value, axis, [(i, i ^ mask) for i in range(size)])


def side(bit):
    axis, mask = bit
    return (lax.axis_index(axis) // mask) % 2


def halve(value, bit):
    rows = value.shape[0] // 2
    mine = side(bit)
    keep = lax.dynamic_slice_in_dim(value, mine * rows, rows, 0)
    give = lax.dynamic_slice_in_dim(value, (1 - mine) * rows, rows, 0)
    return keep + swap(give, bit)


def double(value, bit):
    return value + swap(value, bit)


def gather(value, bit):
    other = swap(value, bit)
    first = side(bit) == 0
    return jnp.concatenate([jnp.where(first, value, other), jnp.where(first, other, value)], axis=0)


def mesh_bits():
    def masks(axis):
        size, mask, found = lax.axis_size(axis), 1, []
        while mask < size:
            found.append((axis, mask))
            mask *= 2
        return found
    col, row = masks("col"), masks("row")
    near = [col[1], col[2], row[0]]
    return col[0], near, col[3:] + row[1:]


def cut(rows, parts, unit):
    base = rows // unit // parts
    extra = rows // unit - base * parts
    return [(base + (1 if i < extra else 0)) * unit for i in range(parts)]


def split_rows(value, sizes):
    out, at = [], 0
    for size in sizes:
        out.append(lax.slice_in_dim(value, at, at + size, axis=0))
        at += size
    return out


def spread_block(masked):
    core, near, far = mesh_bits()
    half = halve(masked, core)
    parts = split_rows(half, cut(half.shape[0], 3, 32))
    out = []
    for i, part in enumerate(parts):
        order = near[i:] + near[:i]
        at = order.index(near[2])
        order = order[: at + 1] + far + order[at + 1 :]
        part = halve(part, order[0])
        for bit in order[1:]:
            part = double(part, bit)
        out.append(gather(part, order[0]))
    return gather(jnp.concatenate(out, axis=0), core)


def sum_all(value):
    core, near, far = mesh_bits()
    half = halve(value, core)
    sizes = cut(half.shape[0], 3, 64)
    parts = split_rows(half, sizes)
    for step in range(3):
        parts = [halve(part, near[(i + step) % 3]) for i, part in enumerate(parts)]
    whole = jnp.concatenate(parts, axis=0)
    for bit in far:
        whole = double(whole, bit)
    parts = split_rows(whole, [size // 8 for size in sizes])
    for step in (2, 1, 0):
        parts = [gather(part, near[(i + step) % 3]) for i, part in enumerate(parts)]
    return gather(jnp.concatenate(parts, axis=0), core)


def tile_at(blocks, row, col):
    return row * blocks - row * (row - 1) // 2 + col - row


def products_kernel(kernel_ref, low_ref, coef_ref, weight_ref, out_ref):
    size = kernel_ref.shape[1]
    blocks = size // TILE
    outs = low_ref.shape[1] // TILE
    step = 2 * TILE
    upper = blocks * (blocks + 1) // 2
    for i in range(size // step):
        left = kernel_ref[:, i * step : (i + 1) * step]
        part = lax.dot_general(left, kernel_ref[:, i * step :], (((0,), (0,)), ((), ())), preferred_element_type=f32)
        for a in range(2):
            row = 2 * i + a
            for col in range(row, blocks):
                at = tile_at(blocks, row, col) * TILE
                lanes = (col - 2 * i) * TILE
                out_ref[at : at + TILE, :] = part[a * TILE : (a + 1) * TILE, lanes : lanes + TILE]
        grad = lax.dot_general(left, low_ref[...], (((0,), (0,)), ((), ())), preferred_element_type=f32)
        grad = grad - weight_ref[0] * coef_ref[i * step : (i + 1) * step, :]
        for a in range(2):
            for b in range(outs):
                at = (upper + (2 * i + a) * outs + b) * TILE
                out_ref[at : at + TILE, :] = grad[a * TILE : (a + 1) * TILE, b * TILE : (b + 1) * TILE]


def products(kernel, low, own_coef, weight):
    size = kernel.shape[1]
    blocks, outs = size // TILE, low.shape[1] // TILE
    tiles = blocks * (blocks + 1) // 2 + blocks * outs
    vmem = pl.BlockSpec(memory_space=pltpu.VMEM)
    return pl.pallas_call(
        products_kernel,
        out_shape=jax.ShapeDtypeStruct((tiles * TILE, TILE), f32),
        in_specs=[vmem, vmem, vmem, pl.BlockSpec(memory_space=pltpu.SMEM)],
        out_specs=vmem,
        compiler_params=pltpu.CompilerParams(vmem_limit_bytes=40 << 20),
    )(kernel, low, own_coef, weight.reshape(1))


def split_three(value):
    high = value.astype(bf16).astype(f32)
    rest = value - high
    middle = rest.astype(bf16).astype(f32)
    return high, middle, rest - middle


def small_inverse(rows, at):
    block = [[None] * SUB for _ in range(SUB)]
    for i in range(SUB):
        for c in range(i, SUB):
            block[i][c] = jnp.broadcast_to(rows[i : i + 1, at + c : at + c + 1], (SUB, TILE))
    inverse = [[None] * SUB for _ in range(SUB)]
    for j in range(SUB):
        root = lax.rsqrt(block[j][j])
        upper = {k: block[j][k] * root for k in range(j + 1, SUB)}
        for k in range(j + 1, SUB):
            for c in range(k, SUB):
                block[k][c] = block[k][c] - upper[k] * upper[c]
        for i in range(j):
            inverse[j][i] = inverse[j][i] * root
        inverse[j][j] = root
        for k in range(j + 1, SUB):
            for i in range(j + 1):
                term = upper[k] * inverse[j][i]
                inverse[k][i] = -term if inverse[k][i] is None else inverse[k][i] - term
    return inverse


def factor_step(pair, inverse_ref, j):
    at = j * SUB
    rows = pair[at : at + SUB, :]
    small = small_inverse(rows, at)
    place = lax.broadcasted_iota(jnp.int32, (SUB, TILE), 0)
    upper = None
    for m in range(SUB):
        column = jnp.zeros((SUB, TILE), f32)
        for i in range(m, SUB):
            column = jnp.where(place == i, small[i][m], column)
        column = jnp.concatenate([column, column], axis=1)
        term = column * jnp.broadcast_to(rows[m : m + 1, :], (SUB, 2 * TILE))
        upper = term if upper is None else upper + term
    inverse_ref[at : at + SUB, :] = upper[:, TILE:]
    if at + SUB < TILE:
        high, middle, low = split_three(upper)
        left = jnp.concatenate([high, high, middle, high, low, middle], axis=0)[:, :TILE].astype(bf16)
        right = jnp.concatenate([high, middle, high, low, high, middle], axis=0).astype(bf16)
        change = lax.dot_general(left, right, (((0,), (0,)), ((), ())), preferred_element_type=f32)
        pair[at + SUB :, :] = pair[at + SUB :, :] - change[at + SUB :, :]


def dot_high(left, right, dims):
    return lax.dot_general(left, right, (dims, ((), ())), precision=HIGHEST, preferred_element_type=f32)


def solve_kernel(total, packed_ref, out_ref, system, pair, inverses):
    size, outs = out_ref.shape
    blocks = size // TILE
    upper = blocks * (blocks + 1) // 2
    scale = 1.0 / total
    for row in range(blocks):
        for col in range(row, blocks):
            at = tile_at(blocks, row, col) * TILE
            system[row * TILE : (row + 1) * TILE, col * TILE : (col + 1) * TILE] = packed_ref[at : at + TILE, :] * scale
        for b in range(outs // TILE):
            at = (upper + row * (outs // TILE) + b) * TILE
            lanes = size + b * TILE
            system[row * TILE : (row + 1) * TILE, lanes : lanes + TILE] = packed_ref[at : at + TILE, :] * scale
        if row:
            system[row * TILE : (row + 1) * TILE, : row * TILE] = jnp.zeros((TILE, row * TILE), f32)
    unit = jnp.where(
        lax.broadcasted_iota(jnp.int32, (TILE, TILE), 0) == lax.broadcasted_iota(jnp.int32, (TILE, TILE), 1), 1.0, 0.0
    ).astype(f32)

    def forward(k, _):
        here = pl.ds(pl.multiple_of(k * TILE, TILE), TILE)
        pair[:, :TILE] = system[here, here] + ridge * unit
        pair[:, TILE:] = unit
        for j in range(TILE // SUB):
            factor_step(pair, inverses.at[k], j)
        system[here, :] = dot_high(inverses[k], system[here, :], ((1,), (0,)))

        def eliminate(i, _):
            there = pl.ds(pl.multiple_of(i * TILE, TILE), TILE)
            system[there, :] = system[there, :] - dot_high(system[here, there], system[here, :], ((0,), (0,)))
            return 0

        lax.fori_loop(k + 1, blocks, eliminate, 0)
        return 0

    lax.fori_loop(0, blocks, forward, 0)

    def backward(t, _):
        k = blocks - 1 - t
        here = pl.ds(pl.multiple_of(k * TILE, TILE), TILE)
        found = dot_high(inverses[k], system[here, size:], ((0,), (0,)))
        out_ref[here, :] = found

        def eliminate(i, _):
            there = pl.ds(pl.multiple_of(i * TILE, TILE), TILE)
            system[there, size:] = system[there, size:] - dot_high(system[there, here], found, ((1,), (0,)))
            return 0

        lax.fori_loop(0, k, eliminate, 0)
        return 0

    lax.fori_loop(0, blocks, backward, 0)


def solve(packed, size, outs, total):
    vmem = pl.BlockSpec(memory_space=pltpu.VMEM)
    return pl.pallas_call(
        functools.partial(solve_kernel, total),
        out_shape=jax.ShapeDtypeStruct((size, outs), f32),
        in_specs=[vmem],
        out_specs=vmem,
        scratch_shapes=[
            pltpu.VMEM((size, size + outs), f32),
            pltpu.VMEM((TILE, 2 * TILE), f32),
            pltpu.VMEM((size // TILE, TILE, TILE), f32),
        ],
        compiler_params=pltpu.CompilerParams(vmem_limit_bytes=40 << 20),
    )(packed)


def body(examples, residuals, coefficients, block_index):
    rows_here = examples.shape[0]
    features = examples.shape[1]
    outs = residuals.shape[1]
    per_device = rows_here // BLOCK
    total_examples = rows_here * lax.axis_size(AXES)
    chosen = block_index[0]
    owner_rank = chosen // per_device
    offset = chosen % per_device * BLOCK
    is_owner = owner_rank == lax.axis_index(AXES)
    my_block = lax.dynamic_slice_in_dim(examples, offset, BLOCK, 0)
    block_rows = spread_block(jnp.where(is_owner, my_block, 0).astype(examples.dtype))
    sq_rows = jnp.sum(jnp.square(examples.astype(f32)), axis=1)
    sq_block = jnp.sum(jnp.square(block_rows.astype(f32)), axis=1)
    inner = lax.dot_general(examples, block_rows, (((1,), (1,)), ((), ())), preferred_element_type=f32)
    kernel = jnp.exp(
        -width_factor * (sq_rows[:, None] + sq_block[None, :] - 2.0 * inner) / features
    ).astype(bf16)
    own_coef = lax.dynamic_slice_in_dim(coefficients, offset, BLOCK, 0)
    weight_own = jnp.where(is_owner, total_examples * ridge, 0.0).astype(f32)
    packed = products(kernel, residuals.astype(bf16), own_coef, weight_own)
    update = solve(sum_all(packed), BLOCK, outs, total_examples)
    update_low = update.astype(bf16)
    new_residuals = residuals - jnp.dot(kernel, update_low, preferred_element_type=f32)
    updated = lax.dynamic_update_slice_in_dim(coefficients, own_coef + update, offset, 0)
    new_coefficients = jnp.where(is_owner, updated, coefficients)
    return (new_residuals, new_coefficients)


def solution(mesh):
    in_specs = (P(("row", "col"), None), P(("row", "col"), None), P(("row", "col"), None), P())
    out_specs = (P(("row", "col"), None), P(("row", "col"), None))
    return jax.shard_map(body, mesh=mesh, in_specs=in_specs, out_specs=out_specs, check_vma=False)
```

```python
import functools

import jax
import jax.numpy as jnp
from jax import lax
from jax.experimental import pallas as pl
from jax.experimental.pallas import tpu as pltpu
from jax.sharding import PartitionSpec as P

BLOCK = 1024
TILE = 128
SUB = 8
AXES = ("row", "col")

ridge = 0.001
width_factor = 0.5
f32 = jnp.float32
bf16 = jnp.bfloat16


def swap(value, bit):
    axis, mask = bit
    size = lax.axis_size(axis)
    return lax.ppermute(value, axis, [(i, i ^ mask) for i in range(size)])


def side(bit):
    axis, mask = bit
    return (lax.axis_index(axis) // mask) % 2


def halve(value, bit):
    rows = value.shape[0] // 2
    mine = side(bit)
    keep = lax.dynamic_slice_in_dim(value, mine * rows, rows, 0)
    give = lax.dynamic_slice_in_dim(value, (1 - mine) * rows, rows, 0)
    return keep + swap(give, bit)


def double(value, bit):
    return value + swap(value, bit)


def gather(value, bit):
    other = swap(value, bit)
    first = side(bit) == 0
    return jnp.concatenate([jnp.where(first, value, other), jnp.where(first, other, value)], axis=0)


def mesh_bits():
    def masks(axis):
        size, mask, found = lax.axis_size(axis), 1, []
        while mask < size:
            found.append((axis, mask))
            mask *= 2
        return found
    col, row = masks("col"), masks("row")
    near = [col[1], col[2], row[0]]
    return col[0], near, col[3:] + row[1:]


def cut(rows, parts, unit):
    base = rows // unit // parts
    extra = rows // unit - base * parts
    return [(base + (1 if i < extra else 0)) * unit for i in range(parts)]


def split_rows(value, sizes):
    out, at = [], 0
    for size in sizes:
        out.append(lax.slice_in_dim(value, at, at + size, axis=0))
        at += size
    return out


def spread_block(masked):
    core, near, far = mesh_bits()
    half = halve(masked, core)
    parts = split_rows(half, cut(half.shape[0], 3, 32))
    out = []
    for i, part in enumerate(parts):
        order = near[i:] + near[:i]
        at = order.index(near[2])
        order = order[: at + 1] + far + order[at + 1 :]
        part = halve(part, order[0])
        for bit in order[1:]:
            part = double(part, bit)
        out.append(gather(part, order[0]))
    return gather(jnp.concatenate(out, axis=0), core)


def sum_all(value):
    core, near, far = mesh_bits()
    half = halve(value, core)
    sizes = cut(half.shape[0], 3, 64)
    parts = split_rows(half, sizes)
    for step in range(3):
        parts = [halve(part, near[(i + step) % 3]) for i, part in enumerate(parts)]
    whole = jnp.concatenate(parts, axis=0)
    for bit in far:
        whole = double(whole, bit)
    parts = split_rows(whole, [size // 8 for size in sizes])
    for step in (2, 1, 0):
        parts = [gather(part, near[(i + step) % 3]) for i, part in enumerate(parts)]
    return gather(jnp.concatenate(parts, axis=0), core)


def tile_at(blocks, row, col):
    return row * blocks - row * (row - 1) // 2 + col - row


def products_kernel(kernel_ref, low_ref, coef_ref, weight_ref, out_ref):
    size = kernel_ref.shape[1]
    blocks = size // TILE
    outs = low_ref.shape[1] // TILE
    step = 2 * TILE
    upper = blocks * (blocks + 1) // 2
    for i in range(size // step):
        left = kernel_ref[:, i * step : (i + 1) * step]
        part = lax.dot_general(left, kernel_ref[:, i * step :], (((0,), (0,)), ((), ())), preferred_element_type=f32)
        for a in range(2):
            row = 2 * i + a
            for col in range(row, blocks):
                at = tile_at(blocks, row, col) * TILE
                lanes = (col - 2 * i) * TILE
                out_ref[at : at + TILE, :] = part[a * TILE : (a + 1) * TILE, lanes : lanes + TILE]
        grad = lax.dot_general(left, low_ref[...], (((0,), (0,)), ((), ())), preferred_element_type=f32)
        grad = grad - weight_ref[0] * coef_ref[i * step : (i + 1) * step, :]
        for a in range(2):
            for b in range(outs):
                at = (upper + (2 * i + a) * outs + b) * TILE
                out_ref[at : at + TILE, :] = grad[a * TILE : (a + 1) * TILE, b * TILE : (b + 1) * TILE]


def products(kernel, low, own_coef, weight):
    size = kernel.shape[1]
    blocks, outs = size // TILE, low.shape[1] // TILE
    tiles = blocks * (blocks + 1) // 2 + blocks * outs
    vmem = pl.BlockSpec(memory_space=pltpu.VMEM)
    return pl.pallas_call(
        products_kernel,
        out_shape=jax.ShapeDtypeStruct((tiles * TILE, TILE), f32),
        in_specs=[vmem, vmem, vmem, pl.BlockSpec(memory_space=pltpu.SMEM)],
        out_specs=vmem,
        compiler_params=pltpu.CompilerParams(vmem_limit_bytes=40 << 20),
    )(kernel, low, own_coef, weight.reshape(1))


def split_three(value):
    high = value.astype(bf16).astype(f32)
    rest = value - high
    middle = rest.astype(bf16).astype(f32)
    return high, middle, rest - middle


def left_six(value, axis):
    h, m, l = split_three(value)
    return jnp.concatenate([h, h, m, h, l, m], axis=axis).astype(bf16)


def right_six(value):
    h, m, l = split_three(value)
    return jnp.concatenate([h, m, h, l, h, m], axis=0).astype(bf16)


def dot6(left, right):
    return lax.dot_general(left, right, (((1,), (0,)), ((), ())), preferred_element_type=f32)


def spread_entry(rows, i, c):
    return jnp.broadcast_to(rows[i : i + 1, c : c + 1], (SUB, TILE))


def small_inverse(rows, at):
    columns = [jnp.broadcast_to(rows[:, at + c : at + c + 1], (SUB, TILE)) for c in range(SUB)]
    block = [[None] * SUB for _ in range(SUB)]
    for i in range(SUB):
        for c in range(i, SUB):
            block[i][c] = jnp.broadcast_to(columns[c][i : i + 1, :], (SUB, TILE))
    inverse = [[None] * SUB for _ in range(SUB)]
    for j in range(SUB):
        root = lax.rsqrt(block[j][j])
        upper = {k: block[j][k] * root for k in range(j + 1, SUB)}
        for k in range(j + 1, SUB):
            for c in range(k, SUB):
                block[k][c] = block[k][c] - upper[k] * upper[c]
        for i in range(j):
            inverse[j][i] = inverse[j][i] * root
        inverse[j][j] = root
        for k in range(j + 1, SUB):
            for i in range(j + 1):
                term = upper[k] * inverse[j][i]
                inverse[k][i] = -term if inverse[k][i] is None else inverse[k][i] - term
    return inverse


def factor_block(pair, inverse_ref):
    steps = TILE // SUB
    place = lax.broadcasted_iota(jnp.int32, (SUB, TILE), 0)
    lane = lax.broadcasted_iota(jnp.int32, (SUB, TILE), 1)
    lanes = lax.broadcasted_iota(jnp.int32, (TILE, TILE), 1)
    rows = pair[0:SUB, :]
    for j in range(steps):
        at = j * SUB
        small = small_inverse(rows, at)
        rows = jnp.where((lane >= at) & (lane < at + SUB), jnp.where(lane - at == place, 1.0, 0.0), rows)
        upper = None
        for m in range(SUB):
            column = small[SUB - 1][m]
            for i in range(m, SUB - 1):
                column = jnp.where(place == i, small[i][m], column)
            if m:
                column = jnp.where(place < m, 0.0, column)
            term = column * jnp.broadcast_to(rows[m : m + 1, :], (SUB, TILE))
            upper = term if upper is None else upper + term
        inverse_ref[at : at + SUB, :] = jnp.where(lane < at + SUB, upper, 0.0)
        if j + 1 == steps:
            break
        after = pair[at + SUB : at + 2 * SUB, :]
        across = [jnp.broadcast_to(after[:, at + m : at + m + 1], (SUB, TILE)) for m in range(SUB)]
        rows = jnp.where((lane >= at) & (lane < at + SUB), 0.0, after)
        for m in range(SUB):
            column = small[m][0] * across[0]
            for i in range(1, m + 1):
                column = column + small[m][i] * across[i]
            rows = rows - column * jnp.broadcast_to(upper[m : m + 1, :], (SUB, TILE))
        if j + 2 < steps:
            h, m, l = split_three(upper)
            left = jnp.concatenate([h, h, m, h, l, m], axis=0).astype(bf16)
            right = jnp.concatenate([h, m, h, l, h, m], axis=0).astype(bf16)
            change = lax.dot_general(left, right, (((0,), (0,)), ((), ())), preferred_element_type=f32)
            below = slice(at + 2 * SUB, TILE)
            here = lanes[below]
            pair[below, :] = jnp.where((here >= at) & (here < at + SUB), 0.0, pair[below, :]) - change[below]


def solve_kernel(total, packed_ref, out_ref, system, pair, inverses):
    size, outs = out_ref.shape
    width = size + outs
    blocks = size // TILE
    upper = blocks * (blocks + 1) // 2
    scale = 1.0 / total
    for row in range(blocks):
        for col in range(row, blocks):
            at = tile_at(blocks, row, col) * TILE
            system[row * TILE : (row + 1) * TILE, col * TILE : (col + 1) * TILE] = packed_ref[at : at + TILE, :] * scale
        for b in range(outs // TILE):
            at = (upper + row * (outs // TILE) + b) * TILE
            lanes = size + b * TILE
            system[row * TILE : (row + 1) * TILE, lanes : lanes + TILE] = packed_ref[at : at + TILE, :] * scale
    unit = jnp.where(
        lax.broadcasted_iota(jnp.int32, (TILE, TILE), 0) == lax.broadcasted_iota(jnp.int32, (TILE, TILE), 1), 1.0, 0.0
    ).astype(f32)

    def forward(k, _):
        here = pl.ds(pl.multiple_of(k * TILE, TILE), TILE)
        pair[...] = system[here, here] + ridge * unit
        factor_block(pair, inverses.at[k])
        for kk in range(blocks):

            @pl.when(k == kk)
            def _(kk=kk):
                first = (kk + 1) * TILE
                mine = slice(kk * TILE, first)
                found = dot6(left_six(inverses[kk], 1), right_six(system[mine, first:]))
                system[mine, first:] = found
                if kk + 1 < blocks:
                    right = right_six(found)
                    left = left_six(found[:, : size - first].T, 1)
                    for at in range(first, size, 2 * TILE):
                        end = min(at + 2 * TILE, size)
                        system[at:end, at:] = system[at:end, at:] - dot6(left[at - first : end - first], right[:, at - first :])
        return 0

    lax.fori_loop(0, blocks, forward, 0)
    for k in reversed(range(blocks)):
        mine = slice(k * TILE, (k + 1) * TILE)
        found = dot6(left_six(inverses[k].T, 1), right_six(system[mine, size:]))
        out_ref[mine, :] = found
        if k:
            left = left_six(system[: k * TILE, mine], 1)
            system[: k * TILE, size:] = system[: k * TILE, size:] - dot6(left, right_six(found))


def solve(packed, size, outs, total):
    vmem = pl.BlockSpec(memory_space=pltpu.VMEM)
    return pl.pallas_call(
        functools.partial(solve_kernel, total),
        out_shape=jax.ShapeDtypeStruct((size, outs), f32),
        in_specs=[vmem],
        out_specs=vmem,
        scratch_shapes=[
            pltpu.VMEM((size, size + outs), f32),
            pltpu.VMEM((TILE, TILE), f32),
            pltpu.VMEM((size // TILE, TILE, TILE), f32),
        ],
        compiler_params=pltpu.CompilerParams(vmem_limit_bytes=48 << 20),
    )(packed)


def body(examples, residuals, coefficients, block_index):
    rows_here = examples.shape[0]
    features = examples.shape[1]
    outs = residuals.shape[1]
    per_device = rows_here // BLOCK
    total_examples = rows_here * lax.axis_size(AXES)
    chosen = block_index[0]
    owner_rank = chosen // per_device
    offset = chosen % per_device * BLOCK
    is_owner = owner_rank == lax.axis_index(AXES)
    my_block = lax.dynamic_slice_in_dim(examples, offset, BLOCK, 0)
    block_rows = spread_block(jnp.where(is_owner, my_block, 0).astype(examples.dtype))
    sq_rows = jnp.sum(jnp.square(examples.astype(f32)), axis=1)
    sq_block = jnp.sum(jnp.square(block_rows.astype(f32)), axis=1)
    inner = lax.dot_general(examples, block_rows, (((1,), (1,)), ((), ())), preferred_element_type=f32)
    kernel = jnp.exp(
        -width_factor * (sq_rows[:, None] + sq_block[None, :] - 2.0 * inner) / features
    ).astype(bf16)
    own_coef = lax.dynamic_slice_in_dim(coefficients, offset, BLOCK, 0)
    weight_own = jnp.where(is_owner, total_examples * ridge, 0.0).astype(f32)
    packed = products(kernel, residuals.astype(bf16), own_coef, weight_own)
    update = solve(sum_all(packed), BLOCK, outs, total_examples)
    update_low = update.astype(bf16)
    new_residuals = residuals - jnp.dot(kernel, update_low, preferred_element_type=f32)
    updated = lax.dynamic_update_slice_in_dim(coefficients, own_coef + update, offset, 0)
    new_coefficients = jnp.where(is_owner, updated, coefficients)
    return (new_residuals, new_coefficients)


def solution(mesh):
    in_specs = (P(("row", "col"), None), P(("row", "col"), None), P(("row", "col"), None), P())
    out_specs = (P(("row", "col"), None), P(("row", "col"), None))
    return jax.shard_map(body, mesh=mesh, in_specs=in_specs, out_specs=out_specs, check_vma=False)
```

```python
import functools

import jax
import jax.numpy as jnp
from jax import lax
from jax.experimental import pallas as pl
from jax.experimental.pallas import tpu as pltpu
from jax.sharding import PartitionSpec as P

BLOCK = 1024
TILE = 128
SUB = 8
AXES = ("row", "col")

ridge = 0.001
width_factor = 0.5
f32 = jnp.float32
bf16 = jnp.bfloat16


def rank_bits():
    def masks(size, unit):
        found = []
        while size > 1:
            found.append(unit)
            unit, size = unit * 2, size // 2
        return found
    columns = lax.axis_size("col")
    col, row = masks(columns, 1), masks(lax.axis_size("row"), columns)
    return col[0], (col[1], col[2], row[0]), col[3:] + row[1:]


def swap(value, pick):
    size = lax.axis_size(AXES)
    return lax.ppermute(value, AXES, [(i, i ^ pick[i % 2]) for i in range(size)])


def is_high(pick):
    rank = lax.axis_index(AXES)
    mask = jnp.where(rank % 2 == 0, pick[0], pick[1])
    return (rank // mask) % 2


def halve(value, pick):
    rows = value.shape[0] // 2
    high = is_high(pick)
    keep = lax.dynamic_slice_in_dim(value, high * rows, rows, 0)
    give = lax.dynamic_slice_in_dim(value, (1 - high) * rows, rows, 0)
    return keep + swap(give, pick)


def gather(value, pick):
    other = swap(value, pick)
    low = is_high(pick) == 0
    return jnp.concatenate([jnp.where(low, value, other), jnp.where(low, other, value)], axis=0)


def sum_all(value, axis, cut, beside=()):
    core, (x, y, z), far = rank_bits()
    half = halve(value, (core, core))
    parts = [lax.slice_in_dim(half, 0, cut, axis=axis), lax.slice_in_dim(half, cut, half.shape[axis], axis=axis)]
    orders = [[(x, y), (y, z), (z, x)], [(z, z), (x, x), (y, y)]]
    for step in range(3):
        parts = [halve(part, order[step]) for part, order in zip(parts, orders)]
        if step == 0 and beside:
            parts, beside = lax.optimization_barrier((parts, beside))
    sizes = [part.shape[axis] for part in parts]
    whole = jnp.concatenate(parts, axis=axis)
    for mask in far:
        whole = whole + swap(whole, (mask, mask))
    parts = [lax.slice_in_dim(whole, 0, sizes[0], axis=axis), lax.slice_in_dim(whole, sizes[0], sum(sizes), axis=axis)]
    for step in (2, 1, 0):
        parts = [gather(part, order[step]) for part, order in zip(parts, orders)]
    return gather(jnp.concatenate(parts, axis=axis), (core, core)), beside


def tile_at(blocks, row, col):
    return row * blocks - row * (row - 1) // 2 + col - row


def products_kernel(kernel_ref, low_ref, coef_ref, weight_ref, out_ref):
    size = kernel_ref.shape[1]
    blocks = size // TILE
    outs = low_ref.shape[1] // TILE
    step = 2 * TILE
    upper = blocks * (blocks + 1) // 2
    for i in range(size // step):
        left = kernel_ref[:, i * step : (i + 1) * step]
        part = lax.dot_general(left, kernel_ref[:, i * step :], (((0,), (0,)), ((), ())), preferred_element_type=f32)
        for a in range(2):
            row = 2 * i + a
            for col in range(row, blocks):
                at = tile_at(blocks, row, col) * TILE
                lanes = (col - 2 * i) * TILE
                out_ref[at : at + TILE, :] = part[a * TILE : (a + 1) * TILE, lanes : lanes + TILE]
        grad = lax.dot_general(left, low_ref[...], (((0,), (0,)), ((), ())), preferred_element_type=f32)
        grad = grad - weight_ref[0] * coef_ref[i * step : (i + 1) * step, :]
        for a in range(2):
            for b in range(outs):
                at = (upper + (2 * i + a) * outs + b) * TILE
                out_ref[at : at + TILE, :] = grad[a * TILE : (a + 1) * TILE, b * TILE : (b + 1) * TILE]


def products(kernel, low, own_coef, weight):
    size = kernel.shape[1]
    blocks, outs = size // TILE, low.shape[1] // TILE
    tiles = blocks * (blocks + 1) // 2 + blocks * outs
    vmem = pl.BlockSpec(memory_space=pltpu.VMEM)
    return pl.pallas_call(
        products_kernel,
        out_shape=jax.ShapeDtypeStruct((tiles * TILE, TILE), f32),
        in_specs=[vmem, vmem, vmem, pl.BlockSpec(memory_space=pltpu.SMEM)],
        out_specs=vmem,
        compiler_params=pltpu.CompilerParams(vmem_limit_bytes=40 << 20),
    )(kernel, low, own_coef, weight.reshape(1))


def split_three(value):
    high = value.astype(bf16).astype(f32)
    rest = value - high
    middle = rest.astype(bf16).astype(f32)
    return high, middle, rest - middle


def left_six(value, axis):
    h, m, l = split_three(value)
    return jnp.concatenate([h, h, m, h, l, m], axis=axis).astype(bf16)


def right_six(value):
    h, m, l = split_three(value)
    return jnp.concatenate([h, m, h, l, h, m], axis=0).astype(bf16)


def dot6(left, right):
    return lax.dot_general(left, right, (((1,), (0,)), ((), ())), preferred_element_type=f32)


def down(value, row):
    return jnp.broadcast_to(value[row : row + 1, :], (SUB, TILE))


def across(value, lane):
    return jnp.broadcast_to(value[:, lane : lane + 1], (SUB, TILE))


def factor_block(pair, inverse_ref):
    steps = TILE // SUB
    place = lax.broadcasted_iota(jnp.int32, (SUB, TILE), 0)
    lane = lax.broadcasted_iota(jnp.int32, (SUB, TILE), 1)
    lanes = lax.broadcasted_iota(jnp.int32, (TILE, TILE), 1)
    rows = pair[0:SUB, :]
    near = pair[SUB : 2 * SUB, :]
    corner = [across(rows, c) for c in range(SUB)]
    for j in range(steps):
        at = j * SUB
        inside = (lane >= at) & (lane < at + SUB)
        block = [[down(corner[c], i) if i <= c else None for c in range(SUB)] for i in range(SUB)]
        rows = jnp.where(inside, jnp.where(lane - at == place, 1.0, 0.0), rows)
        flat = [down(rows, i) for i in range(SUB)]
        lower = []
        if j + 1 < steps:
            lower.append(near)
            corner = [across(near, at + SUB + c) for c in range(SUB)]
        if j + 2 < steps:
            lower.append(pair[at + 2 * SUB : at + 3 * SUB, :])
        tall = [[across(group, at + i) for i in range(SUB)] for group in lower]
        lower = [jnp.where(inside, 0.0, group) for group in lower]
        for p in range(SUB):
            if p % 2 == 0:
                root = lax.rsqrt(block[p][p])
                cross = block[p][p + 1]
                other = lax.rsqrt(block[p][p] * block[p + 1][p + 1] - cross * cross) * (block[p][p] * root)
            else:
                root = other
            upper = {k: block[p][k] * root for k in range(p + 1, SUB)}
            flat[p] = flat[p] * root
            for group in tall:
                group[p] = group[p] * root
            for k in range(p + 1, SUB):
                for c in range(k, SUB):
                    block[k][c] = block[k][c] - upper[k] * upper[c]
                flat[k] = flat[k] - upper[k] * flat[p]
                for group in tall:
                    group[k] = group[k] - upper[k] * group[p]
            if lower:
                corner = [corner[c] - tall[0][p] * down(tall[0][p], c) for c in range(SUB)]
            lower = [group - high[p] * flat[p] for group, high in zip(lower, tall)]
        found = flat[SUB - 1]
        for i in range(SUB - 1):
            found = jnp.where(place == i, flat[i], found)
        inverse_ref[at : at + SUB, :] = jnp.where(lane < at + SUB, found, 0.0)
        if j + 3 < steps:
            h, m, l = split_three(found)
            left = jnp.concatenate([h, h, m, h, l, m], axis=0).astype(bf16)
            right = jnp.concatenate([h, m, h, l, h, m], axis=0).astype(bf16)
            change = lax.dot_general(left, right, (((0,), (0,)), ((), ())), preferred_element_type=f32)
            below = slice(at + 3 * SUB, TILE)
            here = lanes[below]
            pair[below, :] = jnp.where((here >= at) & (here < at + SUB), 0.0, pair[below, :]) - change[below]
        if lower:
            rows = lower[0]
        if len(lower) > 1:
            near = lower[1]


def solve_kernel(total, packed_ref, out_ref, system, pair, inverses):
    size, outs = out_ref.shape
    width = size + outs
    blocks = size // TILE
    upper = blocks * (blocks + 1) // 2
    scale = 1.0 / total
    for row in range(blocks):
        for col in range(row, blocks):
            at = tile_at(blocks, row, col) * TILE
            system[row * TILE : (row + 1) * TILE, col * TILE : (col + 1) * TILE] = packed_ref[at : at + TILE, :] * scale
        for b in range(outs // TILE):
            at = (upper + row * (outs // TILE) + b) * TILE
            lanes = size + b * TILE
            system[row * TILE : (row + 1) * TILE, lanes : lanes + TILE] = packed_ref[at : at + TILE, :] * scale
    unit = jnp.where(
        lax.broadcasted_iota(jnp.int32, (TILE, TILE), 0) == lax.broadcasted_iota(jnp.int32, (TILE, TILE), 1), 1.0, 0.0
    ).astype(f32)

    def forward(k, _):
        here = pl.ds(pl.multiple_of(k * TILE, TILE), TILE)
        pair[...] = system[here, here] + ridge * unit
        factor_block(pair, inverses.at[k])
        for kk in range(blocks):

            @pl.when(k == kk)
            def _(kk=kk):
                first = (kk + 1) * TILE
                mine = slice(kk * TILE, first)
                found = dot6(left_six(inverses[kk], 1), right_six(system[mine, first:]))
                system[mine, first:] = found
                if kk + 1 < blocks:
                    right = right_six(found)
                    left = left_six(found[:, : size - first].T, 1)
                    for at in range(first, size, 2 * TILE):
                        end = min(at + 2 * TILE, size)
                        system[at:end, at:] = system[at:end, at:] - dot6(left[at - first : end - first], right[:, at - first :])
        return 0

    lax.fori_loop(0, blocks, forward, 0)
    for k in reversed(range(blocks)):
        mine = slice(k * TILE, (k + 1) * TILE)
        found = dot6(left_six(inverses[k].T, 1), right_six(system[mine, size:]))
        out_ref[mine, :] = found
        if k:
            left = left_six(system[: k * TILE, mine], 1)
            system[: k * TILE, size:] = system[: k * TILE, size:] - dot6(left, right_six(found))


def solve(packed, size, outs, total):
    vmem = pl.BlockSpec(memory_space=pltpu.VMEM)
    return pl.pallas_call(
        functools.partial(solve_kernel, total),
        out_shape=jax.ShapeDtypeStruct((size, outs), f32),
        in_specs=[vmem],
        out_specs=vmem,
        scratch_shapes=[
            pltpu.VMEM((size, size + outs), f32),
            pltpu.VMEM((TILE, TILE), f32),
            pltpu.VMEM((size // TILE, TILE, TILE), f32),
        ],
        compiler_params=pltpu.CompilerParams(vmem_limit_bytes=48 << 20),
    )(packed)


def body(examples, residuals, coefficients, block_index):
    rows_here = examples.shape[0]
    features = examples.shape[1]
    outs = residuals.shape[1]
    per_device = rows_here // BLOCK
    total_examples = rows_here * lax.axis_size(AXES)
    chosen = block_index[0]
    owner_rank = chosen // per_device
    offset = chosen % per_device * BLOCK
    is_owner = owner_rank == lax.axis_index(AXES)
    my_block = lax.dynamic_slice_in_dim(examples, offset, BLOCK, 0)
    masked = jnp.where(is_owner, my_block, 0).astype(examples.dtype)
    sq_rows = jnp.sum(jnp.square(examples.astype(f32)), axis=1)
    low = residuals.astype(bf16)
    block_rows, (sq_rows, low, coefficients) = sum_all(
        masked, 1, features * 5 // 8 // TILE * TILE, (sq_rows, low, coefficients)
    )
    sq_block = jnp.sum(jnp.square(block_rows.astype(f32)), axis=1)
    inner = lax.dot_general(examples, block_rows, (((1,), (1,)), ((), ())), preferred_element_type=f32)
    kernel = jnp.exp(
        -width_factor * (sq_rows[:, None] + sq_block[None, :] - 2.0 * inner) / features
    ).astype(bf16)
    own_coef = lax.dynamic_slice_in_dim(coefficients, offset, BLOCK, 0)
    weight_own = jnp.where(is_owner, total_examples * ridge, 0.0).astype(f32)
    packed = products(kernel, low, own_coef, weight_own)
    unit = 8 * SUB
    sums, _ = sum_all(packed, 0, packed.shape[0] // 2 * 2 // 3 // unit * unit)
    update = solve(sums, BLOCK, outs, total_examples)
    update_low = update.astype(bf16)
    new_residuals = residuals - jnp.dot(kernel, update_low, preferred_element_type=f32)
    stacked = coefficients.reshape(per_device, BLOCK, outs)
    place = lax.broadcasted_iota(jnp.int32, (per_device, 1, 1), 0)
    touched = is_owner & (place == chosen % per_device)
    new_coefficients = jnp.where(touched, stacked + update, stacked).reshape(rows_here, outs)
    return (new_residuals, new_coefficients)


def solution(mesh):
    in_specs = (P(("row", "col"), None), P(("row", "col"), None), P(("row", "col"), None), P())
    out_specs = (P(("row", "col"), None), P(("row", "col"), None))
    return jax.shard_map(body, mesh=mesh, in_specs=in_specs, out_specs=out_specs, check_vma=False)
```

```python
import functools

import jax
import jax.numpy as jnp
from jax import lax
from jax.experimental import pallas as pl
from jax.experimental.pallas import tpu as pltpu
from jax.sharding import PartitionSpec as P

BLOCK = 1024
TILE = 128
SUB = 8
AXES = ("row", "col")

ridge = 0.001
width_factor = 0.5
f32 = jnp.float32
bf16 = jnp.bfloat16


def rank_bits():
    def masks(size, unit):
        found = []
        while size > 1:
            found.append(unit)
            unit, size = unit * 2, size // 2
        return found
    columns = lax.axis_size("col")
    col, row = masks(columns, 1), masks(lax.axis_size("row"), columns)
    return col[0], (col[1], col[2], row[0]), col[3:] + row[1:]


def swap(value, pick):
    size = lax.axis_size(AXES)
    return lax.ppermute(value, AXES, [(i, i ^ pick[i % 2]) for i in range(size)])


def is_high(pick):
    rank = lax.axis_index(AXES)
    mask = jnp.where(rank % 2 == 0, pick[0], pick[1])
    return (rank // mask) % 2


def halve(value, pick):
    rows = value.shape[0] // 2
    high = is_high(pick)
    keep = lax.dynamic_slice_in_dim(value, high * rows, rows, 0)
    give = lax.dynamic_slice_in_dim(value, (1 - high) * rows, rows, 0)
    return keep + swap(give, pick)


def in_order(value, other, pick):
    low = is_high(pick) == 0
    return jnp.concatenate([jnp.where(low, value, other), jnp.where(low, other, value)], axis=0)


def sum_parts(give, keep, axis, cuts=(), beside=()):
    core, (x, y, z), far = rank_bits()
    both = (core, core)
    if cuts:
        orders = [[(x, y), (y, z), (z, x)], [(z, z), (x, x), (y, y)]]
    else:
        orders = [[(x, x), (y, y), (z, z)], [(y, y), (z, z), (x, x)], [(z, z), (x, x), (y, y)]]
    if cuts:
        whole = keep[0] + swap(give[0], both)
        parts = [lax.slice_in_dim(whole, low, high, axis=axis) for low, high in cuts]
    else:
        moved = [swap(part, both) for part in give]
        parts = [part + other for part, other in zip(keep, moved)]
    for step in range(3):
        parts = [halve(part, order[step]) for part, order in zip(parts, orders)]
        if step == 0 and beside:
            parts, beside = lax.optimization_barrier((parts, beside))
    ends = [0]
    for part in parts:
        ends.append(ends[-1] + part.shape[axis])
    whole = jnp.concatenate(parts, axis=axis)
    for mask in far:
        whole = whole + swap(whole, (mask, mask))
    parts = [lax.slice_in_dim(whole, low, high, axis=axis) for low, high in zip(ends, ends[1:])]
    for step in (2, 1, 0):
        parts = [in_order(part, swap(part, order[step]), order[step]) for part, order in zip(parts, orders)]
    if cuts:
        parts = [jnp.concatenate(parts, axis=axis)]
    return parts, [swap(part, both) for part in parts], beside


def half_tiles(blocks, outs, half):
    split = blocks // 2
    rows = range(split) if half == 0 else range(split, blocks)
    tiles = [(row, col) for row in rows for col in range(row, blocks)]
    if half:
        tiles += [(row, blocks + b) for row in range(blocks) for b in range(outs // TILE)]
    return tiles


def part_sizes(blocks, outs):
    tiles = len(half_tiles(blocks, outs, 0))
    assert tiles == len(half_tiles(blocks, outs, 1))
    return [(tiles + 2 - i) // 3 for i in range(3)]


def part_place(sizes, index):
    for part, size in enumerate(sizes):
        if index < size:
            return part, slice(index * TILE, (index + 1) * TILE)
        index -= size


def products_kernel(sizes, core_ref, kernel_ref, low_ref, coef_ref, weight_ref, *refs):
    keep_refs, give_refs, packed = refs[:3], refs[3:6], refs[6]
    size, outs = kernel_ref.shape[1], low_ref.shape[1]
    blocks = size // TILE
    step = 2 * TILE
    contract = (((0,), (0,)), ((), ()))
    tiles = half_tiles(blocks, outs, 0) + half_tiles(blocks, outs, 1)
    place = {tile: slice(index * TILE, (index + 1) * TILE) for index, tile in enumerate(tiles)}

    def put(value, row, col):
        for a in range(value.shape[0] // TILE):
            for b in range(value.shape[1] // TILE):
                if (row + a, col + b) in place:
                    packed[place[row + a, col + b], :] = value[a * TILE : (a + 1) * TILE, b * TILE : (b + 1) * TILE]

    for i in range(size // step):
        left = kernel_ref[:, i * step : (i + 1) * step]
        put(lax.dot_general(left, kernel_ref[:, i * step :], contract, preferred_element_type=f32), 2 * i, 2 * i)
        grad = lax.dot_general(left, low_ref[...], contract, preferred_element_type=f32)
        put(grad - weight_ref[0] * coef_ref[i * step : (i + 1) * step, :], 2 * i, blocks)
    first = core_ref[0] == 0
    start, half = 0, sum(sizes) * TILE
    for part, count in enumerate(sizes):
        rows = count * TILE
        low, high = packed[start : start + rows, :], packed[half + start : half + start + rows, :]
        keep_refs[part][...] = jnp.where(first, low, high)
        give_refs[part][...] = jnp.where(first, high, low)
        start += rows


def products(core, kernel, low, own_coef, weight):
    size, outs = kernel.shape[1], low.shape[1]
    sizes = part_sizes(size // TILE, outs)
    vmem = pl.BlockSpec(memory_space=pltpu.VMEM)
    smem = pl.BlockSpec(memory_space=pltpu.SMEM)
    found = pl.pallas_call(
        functools.partial(products_kernel, sizes),
        out_shape=[jax.ShapeDtypeStruct((count * TILE, TILE), f32) for count in sizes] * 2,
        in_specs=[smem, vmem, vmem, vmem, smem],
        out_specs=[vmem] * 6,
        scratch_shapes=[pltpu.VMEM((2 * sum(sizes) * TILE, TILE), f32)],
        compiler_params=pltpu.CompilerParams(vmem_limit_bytes=24 << 20),
    )(core.reshape(1), kernel, low, own_coef, weight.reshape(1))
    return found[:3], found[3:]


def split_three(value):
    high = value.astype(bf16).astype(f32)
    rest = value - high
    middle = rest.astype(bf16).astype(f32)
    return high, middle, rest - middle


def left_six(value, axis):
    h, m, l = split_three(value)
    return jnp.concatenate([h, h, m, h, l, m], axis=axis).astype(bf16)


def right_six(value):
    h, m, l = split_three(value)
    return jnp.concatenate([h, m, h, l, h, m], axis=0).astype(bf16)


def dot6(left, right):
    return lax.dot_general(left, right, (((1,), (0,)), ((), ())), preferred_element_type=f32)


def down(value, row):
    return jnp.broadcast_to(value[row : row + 1, :], (SUB, TILE))


def across(value, lane):
    return jnp.broadcast_to(value[:, lane : lane + 1], (SUB, TILE))


def factor_block(pair, inverse_ref):
    steps = TILE // SUB
    place = lax.broadcasted_iota(jnp.int32, (SUB, TILE), 0)
    lane = lax.broadcasted_iota(jnp.int32, (SUB, TILE), 1)
    lanes = lax.broadcasted_iota(jnp.int32, (TILE, TILE), 1)
    rows = pair[0:SUB, :]
    near = pair[SUB : 2 * SUB, :]
    corner = [across(rows, c) for c in range(SUB)]
    for j in range(steps):
        at = j * SUB
        inside = (lane >= at) & (lane < at + SUB)
        block = corner
        rows = jnp.where(inside, jnp.where(lane - at == place, 1.0, 0.0), rows)
        flat = [down(rows, i) for i in range(SUB)]
        lower = []
        if j + 1 < steps:
            lower.append(near)
            corner = [across(near, at + SUB + c) for c in range(SUB)]
        if j + 2 < steps:
            lower.append(pair[at + 2 * SUB : at + 3 * SUB, :])
        tall = [[across(group, at + i) for i in range(SUB)] for group in lower]
        lower = [jnp.where(inside, 0.0, group) for group in lower]
        for p in range(SUB):
            root = lax.rsqrt(down(block[p], p))
            column = block[p] * root
            upper = {k: down(column, k) for k in range(p + 1, SUB)}
            block = [value - column * upper[c] if c > p else value for c, value in enumerate(block)]
            flat[p] = flat[p] * root
            for group in tall:
                group[p] = group[p] * root
            for k in range(p + 1, SUB):
                flat[k] = flat[k] - upper[k] * flat[p]
                for group in tall:
                    group[k] = group[k] - upper[k] * group[p]
            if lower:
                corner = [corner[c] - tall[0][p] * down(tall[0][p], c) for c in range(SUB)]
            lower = [group - high[p] * flat[p] for group, high in zip(lower, tall)]
        found = flat[SUB - 1]
        for i in range(SUB - 1):
            found = jnp.where(place == i, flat[i], found)
        inverse_ref[at : at + SUB, :] = jnp.where(lane < at + SUB, found, 0.0)
        if j + 3 < steps:
            h, m, l = split_three(found)
            left = jnp.concatenate([h, h, m, h, l, m], axis=0).astype(bf16)
            right = jnp.concatenate([h, m, h, l, h, m], axis=0).astype(bf16)
            change = lax.dot_general(left, right, (((0,), (0,)), ((), ())), preferred_element_type=f32)
            below = slice(at + 3 * SUB, TILE)
            here = lanes[below]
            pair[below, :] = jnp.where((here >= at) & (here < at + SUB), 0.0, pair[below, :]) - change[below]
        if lower:
            rows = lower[0]
        if len(lower) > 1:
            near = lower[1]


def solve_kernel(total, core_ref, *refs):
    own_refs, other_refs = refs[:3], refs[3:6]
    out_ref, system, pair, inverses = refs[6:]
    size, outs = out_ref.shape
    width = size + outs
    blocks = size // TILE
    scale = 1.0 / total
    sizes = part_sizes(blocks, outs)
    for half in range(2):
        mine = core_ref[0] == half
        for index, (row, col) in enumerate(half_tiles(blocks, outs, half)):
            part, rows = part_place(sizes, index)
            value = jnp.where(mine, own_refs[part][rows, :], other_refs[part][rows, :])
            system[row * TILE : (row + 1) * TILE, col * TILE : (col + 1) * TILE] = value * scale
    unit = jnp.where(
        lax.broadcasted_iota(jnp.int32, (TILE, TILE), 0) == lax.broadcasted_iota(jnp.int32, (TILE, TILE), 1), 1.0, 0.0
    ).astype(f32)

    def forward(k, _):
        here = pl.ds(pl.multiple_of(k * TILE, TILE), TILE)
        pair[...] = system[here, here] + ridge * unit
        factor_block(pair, inverses.at[k])
        for kk in range(blocks):

            @pl.when(k == kk)
            def _(kk=kk):
                first = (kk + 1) * TILE
                mine = slice(kk * TILE, first)
                found = dot6(left_six(inverses[kk], 1), right_six(system[mine, first:]))
                system[mine, first:] = found
                if kk + 1 < blocks:
                    right = right_six(found)
                    left = left_six(found[:, : size - first].T, 1)
                    for at in range(first, size, 2 * TILE):
                        end = min(at + 2 * TILE, size)
                        system[at:end, at:] = system[at:end, at:] - dot6(left[at - first : end - first], right[:, at - first :])
        return 0

    lax.fori_loop(0, blocks, forward, 0)
    for k in reversed(range(blocks)):
        mine = slice(k * TILE, (k + 1) * TILE)
        found = dot6(left_six(inverses[k].T, 1), right_six(system[mine, size:]))
        out_ref[mine, :] = found
        if k:
            left = left_six(system[: k * TILE, mine], 1)
            system[: k * TILE, size:] = system[: k * TILE, size:] - dot6(left, right_six(found))


def solve(core, own, other, size, outs, total):
    vmem = pl.BlockSpec(memory_space=pltpu.VMEM)
    return pl.pallas_call(
        functools.partial(solve_kernel, total),
        out_shape=jax.ShapeDtypeStruct((size, outs), f32),
        in_specs=[pl.BlockSpec(memory_space=pltpu.SMEM)] + [vmem] * 6,
        out_specs=vmem,
        scratch_shapes=[
            pltpu.VMEM((size, size + outs), f32),
            pltpu.VMEM((TILE, TILE), f32),
            pltpu.VMEM((size // TILE, TILE, TILE), f32),
        ],
        compiler_params=pltpu.CompilerParams(vmem_limit_bytes=24 << 20),
    )(core.reshape(1), *own, *other)


def body(examples, residuals, coefficients, block_index):
    rows_here = examples.shape[0]
    features = examples.shape[1]
    outs = residuals.shape[1]
    per_device = rows_here // BLOCK
    total_examples = rows_here * lax.axis_size(AXES)
    chosen = block_index[0]
    owner_rank = chosen // per_device
    offset = chosen % per_device * BLOCK
    is_owner = owner_rank == lax.axis_index(AXES)
    core_pick = rank_bits()[0], rank_bits()[0]
    core = is_high(core_pick)
    first_width = features * 5 // 8 // TILE * TILE

    whole = jnp.where(is_owner, lax.dynamic_slice_in_dim(examples, offset, BLOCK, 0), 0).astype(examples.dtype)

    def masked(half):
        return lax.dynamic_slice_in_dim(whole, half * (BLOCK // 2), BLOCK // 2, 0)

    sq_rows = jnp.sum(jnp.square(examples.astype(f32)), axis=1)
    low = residuals.astype(bf16)
    cuts = ((0, first_width), (first_width, features))
    (own,), (other,), (sq_rows, low, coefficients) = sum_parts(
        [masked(1 - core)], [masked(core)], 1, cuts, (sq_rows, low, coefficients)
    )
    block_rows = in_order(own, other, core_pick)
    sq_block = jnp.sum(jnp.square(block_rows.astype(f32)), axis=1)
    inner = lax.dot_general(examples, block_rows, (((1,), (1,)), ((), ())), preferred_element_type=f32)
    kernel = jnp.exp(
        -width_factor * (sq_rows[:, None] + sq_block[None, :] - 2.0 * inner) / features
    ).astype(bf16)
    own_coef = lax.dynamic_slice_in_dim(coefficients, offset, BLOCK, 0)
    weight_own = jnp.where(is_owner, total_examples * ridge, 0.0).astype(f32)
    keep, give = products(core, kernel, low, own_coef, weight_own)
    own, other, _ = sum_parts(give, keep, 0)
    update = solve(core, own, other, BLOCK, outs, total_examples)
    update_low = update.astype(bf16)
    new_residuals = residuals - jnp.dot(kernel, update_low, preferred_element_type=f32)
    stacked = coefficients.reshape(per_device, BLOCK, outs)
    place = lax.broadcasted_iota(jnp.int32, (per_device, 1, 1), 0)
    touched = is_owner & (place == chosen % per_device)
    new_coefficients = jnp.where(touched, stacked + update, stacked).reshape(rows_here, outs)
    return (new_residuals, new_coefficients)


def solution(mesh):
    in_specs = (P(("row", "col"), None), P(("row", "col"), None), P(("row", "col"), None), P())
    out_specs = (P(("row", "col"), None), P(("row", "col"), None))
    return jax.shard_map(body, mesh=mesh, in_specs=in_specs, out_specs=out_specs, check_vma=False)
```

```python
import functools

import jax
import jax.numpy as jnp
from jax import lax
from jax.experimental import pallas as pl
from jax.experimental.pallas import tpu as pltpu
from jax.sharding import PartitionSpec as P

BLOCK = 1024
TILE = 128
SUB = 8
STRIP = 512
AXES = ("row", "col")

ridge = 0.001
width_factor = 0.5
f32 = jnp.float32
bf16 = jnp.bfloat16


def rank_bits():
    def masks(size, unit):
        found = []
        while size > 1:
            found.append(unit)
            unit, size = unit * 2, size // 2
        return found
    columns = lax.axis_size("col")
    col, row = masks(columns, 1), masks(lax.axis_size("row"), columns)
    return col[0], (col[1], col[2], row[0]), col[3:] + row[1:]


def swap(value, pick):
    size = lax.axis_size(AXES)
    return lax.ppermute(value, AXES, [(i, i ^ pick[i % 2]) for i in range(size)])


def is_high(pick):
    rank = lax.axis_index(AXES)
    mask = jnp.where(rank % 2 == 0, pick[0], pick[1])
    return (rank // mask) % 2


def halve(value, pick):
    rows = value.shape[0] // 2
    high = is_high(pick)
    keep = lax.dynamic_slice_in_dim(value, high * rows, rows, 0)
    give = lax.dynamic_slice_in_dim(value, (1 - high) * rows, rows, 0)
    return keep + swap(give, pick)


def in_order(value, other, pick):
    low = is_high(pick) == 0
    return jnp.concatenate([jnp.where(low, value, other), jnp.where(low, other, value)], axis=0)


def sum_parts(give, keep, axis, cuts=(), beside=()):
    core, (x, y, z), far = rank_bits()
    both = (core, core)
    if cuts:
        orders = [[(x, y), (y, z), (z, x)], [(z, z), (x, x), (y, y)]]
    else:
        orders = [[(x, x), (y, y), (z, z)], [(y, y), (z, z), (x, x)], [(z, z), (x, x), (y, y)]]
    if cuts:
        whole = keep[0] + swap(give[0], both)
        parts = [lax.slice_in_dim(whole, low, high, axis=axis) for low, high in cuts]
    else:
        moved = [swap(part, both) for part in give]
        parts = [part + other for part, other in zip(keep, moved)]
    for step in range(3):
        parts = [halve(part, order[step]) for part, order in zip(parts, orders)]
        if step == 0 and beside:
            parts, beside = lax.optimization_barrier((parts, beside))
    ends = [0]
    for part in parts:
        ends.append(ends[-1] + part.shape[axis])
    whole = jnp.concatenate(parts, axis=axis)
    for mask in far:
        whole = whole + swap(whole, (mask, mask))
    parts = [lax.slice_in_dim(whole, low, high, axis=axis) for low, high in zip(ends, ends[1:])]
    for step in (2, 1, 0):
        parts = [in_order(part, swap(part, order[step]), order[step]) for part, order in zip(parts, orders)]
    if cuts:
        parts = [jnp.concatenate(parts, axis=axis)]
    return parts, [swap(part, both) for part in parts], beside


def half_tiles(blocks, outs, half):
    split = blocks // 2
    rows = range(split) if half == 0 else range(split, blocks)
    tiles = [(row, col) for row in rows for col in range(row, blocks)]
    if half:
        tiles += [(row, blocks + b) for row in range(blocks) for b in range(outs // TILE)]
    return tiles


def part_sizes(blocks, outs):
    tiles = len(half_tiles(blocks, outs, 0))
    assert tiles == len(half_tiles(blocks, outs, 1))
    return [(tiles + 2 - i) // 3 for i in range(3)]


def part_place(sizes, index):
    for part, size in enumerate(sizes):
        if index < size:
            return part, slice(index * TILE, (index + 1) * TILE)
        index -= size


def products_kernel(sizes, core_ref, kernel_ref, low_ref, coef_ref, weight_ref, *refs):
    keep_refs, give_refs, packed = refs[:3], refs[3:6], refs[6]
    size, outs = kernel_ref.shape[1], low_ref.shape[1]
    blocks = size // TILE
    step = 2 * TILE
    contract = (((0,), (0,)), ((), ()))
    tiles = half_tiles(blocks, outs, 0) + half_tiles(blocks, outs, 1)
    place = {tile: slice(index * TILE, (index + 1) * TILE) for index, tile in enumerate(tiles)}

    def put(value, row, col):
        for a in range(value.shape[0] // TILE):
            for b in range(value.shape[1] // TILE):
                if (row + a, col + b) in place:
                    packed[place[row + a, col + b], :] = value[a * TILE : (a + 1) * TILE, b * TILE : (b + 1) * TILE]

    for i in range(size // step):
        left = kernel_ref[:, i * step : (i + 1) * step]
        put(lax.dot_general(left, kernel_ref[:, i * step :], contract, preferred_element_type=f32), 2 * i, 2 * i)
        grad = lax.dot_general(left, low_ref[...], contract, preferred_element_type=f32)
        put(grad - weight_ref[0] * coef_ref[i * step : (i + 1) * step, :], 2 * i, blocks)
    first = core_ref[0] == 0
    start, half = 0, sum(sizes) * TILE
    for part, count in enumerate(sizes):
        rows = count * TILE
        low, high = packed[start : start + rows, :], packed[half + start : half + start + rows, :]
        keep_refs[part][...] = jnp.where(first, low, high)
        give_refs[part][...] = jnp.where(first, high, low)
        start += rows


def products(core, kernel, low, own_coef, weight):
    size, outs = kernel.shape[1], low.shape[1]
    sizes = part_sizes(size // TILE, outs)
    vmem = pl.BlockSpec(memory_space=pltpu.VMEM)
    smem = pl.BlockSpec(memory_space=pltpu.SMEM)
    found = pl.pallas_call(
        functools.partial(products_kernel, sizes),
        out_shape=[jax.ShapeDtypeStruct((count * TILE, TILE), f32) for count in sizes] * 2,
        in_specs=[smem, vmem, vmem, vmem, smem],
        out_specs=[vmem] * 6,
        scratch_shapes=[pltpu.VMEM((2 * sum(sizes) * TILE, TILE), f32)],
        compiler_params=pltpu.CompilerParams(vmem_limit_bytes=24 << 20),
    )(core.reshape(1), kernel, low, own_coef, weight.reshape(1))
    return found[:3], found[3:]


def split_three(value):
    high = value.astype(bf16).astype(f32)
    rest = value - high
    middle = rest.astype(bf16).astype(f32)
    return high, middle, rest - middle


def left_six(value, axis):
    h, m, l = split_three(value)
    return jnp.concatenate([h, h, m, h, l, m], axis=axis).astype(bf16)


def right_six(value):
    h, m, l = split_three(value)
    return jnp.concatenate([h, m, h, l, h, m], axis=0).astype(bf16)


def dot6(left, right):
    return lax.dot_general(left, right, (((1,), (0,)), ((), ())), preferred_element_type=f32)


def down(value, row):
    return jnp.broadcast_to(value[row : row + 1, :], (SUB, TILE))


def across(value, lane):
    return jnp.broadcast_to(value[:, lane : lane + 1], (SUB, TILE))


def factor_block(pair, inverse_ref):
    steps = TILE // SUB
    place = lax.broadcasted_iota(jnp.int32, (SUB, TILE), 0)
    lane = lax.broadcasted_iota(jnp.int32, (SUB, TILE), 1)
    lanes = lax.broadcasted_iota(jnp.int32, (TILE, TILE), 1)
    rows = pair[0:SUB, :]
    near = pair[SUB : 2 * SUB, :]
    corner = [across(rows, c) for c in range(SUB)]
    for j in range(steps):
        at = j * SUB
        inside = (lane >= at) & (lane < at + SUB)
        block = corner
        rows = jnp.where(inside, jnp.where(lane - at == place, 1.0, 0.0), rows)
        flat = [down(rows, i) for i in range(SUB)]
        lower = []
        if j + 1 < steps:
            lower.append(near)
            corner = [across(near, at + SUB + c) for c in range(SUB)]
        if j + 2 < steps:
            lower.append(pair[at + 2 * SUB : at + 3 * SUB, :])
        tall = [[across(group, at + i) for i in range(SUB)] for group in lower]
        lower = [jnp.where(inside, 0.0, group) for group in lower]
        for p in range(SUB):
            root = lax.rsqrt(down(block[p], p))
            column = block[p] * root
            upper = {k: down(column, k) for k in range(p + 1, SUB)}
            block = [value - column * upper[c] if c > p else value for c, value in enumerate(block)]
            flat[p] = flat[p] * root
            for group in tall:
                group[p] = group[p] * root
            for k in range(p + 1, SUB):
                flat[k] = flat[k] - upper[k] * flat[p]
                for group in tall:
                    group[k] = group[k] - upper[k] * group[p]
            if lower:
                corner = [corner[c] - tall[0][p] * down(tall[0][p], c) for c in range(SUB)]
            lower = [group - high[p] * flat[p] for group, high in zip(lower, tall)]
        found = flat[SUB - 1]
        for i in range(SUB - 1):
            found = jnp.where(place == i, flat[i], found)
        inverse_ref[at : at + SUB, :] = jnp.where(lane < at + SUB, found, 0.0)
        if j + 3 < steps:
            h, m, l = split_three(found)
            left = jnp.concatenate([h, h, m, h, l, m], axis=0).astype(bf16)
            right = jnp.concatenate([h, m, h, l, h, m], axis=0).astype(bf16)
            change = lax.dot_general(left, right, (((0,), (0,)), ((), ())), preferred_element_type=f32)
            below = slice(at + 3 * SUB, TILE)
            here = lanes[below]
            pair[below, :] = jnp.where((here >= at) & (here < at + SUB), 0.0, pair[below, :]) - change[below]
        if lower:
            rows = lower[0]
        if len(lower) > 1:
            near = lower[1]


def solve_kernel(total, core_ref, place_ref, mine_ref, *refs):
    own_refs, other_refs, (kernel_hbm, residual_hbm, coef_hbm) = refs[:3], refs[3:6], refs[6:9]
    new_residual_hbm, new_coef_hbm, system, pair, inverses, update = refs[9:15]
    kernel_ref, residual_ref, coef_ref, touched, sems = refs[15:]
    copies = [
        pltpu.make_async_copy(source, target, sems.at[at])
        for at, (source, target) in enumerate(
            ((kernel_hbm, kernel_ref), (residual_hbm, residual_ref), (coef_hbm, coef_ref), (coef_ref, new_coef_hbm))
        )
    ]
    for copy in copies[:3]:
        copy.start()
    size, outs = update.shape
    width = size + outs
    blocks = size // TILE
    scale = 1.0 / total
    sizes = part_sizes(blocks, outs)
    for half in range(2):
        mine = core_ref[0] == half
        for index, (row, col) in enumerate(half_tiles(blocks, outs, half)):
            part, rows = part_place(sizes, index)
            value = jnp.where(mine, own_refs[part][rows, :], other_refs[part][rows, :])
            system[row * TILE : (row + 1) * TILE, col * TILE : (col + 1) * TILE] = value * scale
    unit = jnp.where(
        lax.broadcasted_iota(jnp.int32, (TILE, TILE), 0) == lax.broadcasted_iota(jnp.int32, (TILE, TILE), 1), 1.0, 0.0
    ).astype(f32)

    def forward(k, _):
        @pl.when(k == blocks // 2)
        def _():
            copies[2].wait()
            copies[3].start()

        here = pl.ds(pl.multiple_of(k * TILE, TILE), TILE)
        pair[...] = system[here, here] + ridge * unit
        factor_block(pair, inverses.at[k])
        for kk in range(blocks):

            @pl.when(k == kk)
            def _(kk=kk):
                first = (kk + 1) * TILE
                mine = slice(kk * TILE, first)
                inverse = inverses[kk]
                found = dot6(left_six(inverse, 1), right_six(system[mine, first:]))
                right = right_six(found)
                system[mine, first:] = dot6(left_six(inverse.T, 1), right)
                if kk + 1 < blocks:
                    left = left_six(found[:, : size - first].T, 1)
                    for at in range(first, size, 2 * TILE):
                        end = min(at + 2 * TILE, size)
                        system[at:end, at:] = system[at:end, at:] - dot6(left[at - first : end - first], right[:, at - first :])
        return 0

    lax.fori_loop(0, blocks, forward, 0)
    copies[3].wait()
    copies[0].wait()
    copies[1].wait()

    def change_residuals(k, strip):
        lanes = slice(k * TILE, (k + 2) * TILE)
        low = update[lanes, :].astype(bf16)
        change = jnp.dot(kernel_ref[strip, lanes], low, preferred_element_type=f32)
        residual_ref[strip, :] = residual_ref[strip, :] - change

    strips = [slice(at, at + STRIP) for at in range(0, residual_ref.shape[0], STRIP)]
    for k in reversed(range(blocks)):
        mine = slice(k * TILE, (k + 1) * TILE)
        found = system[mine, size:]
        update[mine, :] = found
        if k:
            left = left_six(system[: k * TILE, mine], 1)
            system[: k * TILE, size:] = system[: k * TILE, size:] - dot6(left, right_six(found))
        if k and k % 2 == 0:
            for strip in strips:
                change_residuals(k, strip)
    place = pl.ds(pl.multiple_of(place_ref[0] * size, size), size)
    chosen = coef_ref[place, :]
    touched[...] = jnp.where(mine_ref[0] == 1, chosen + update[...], chosen)
    ends = [pltpu.make_async_copy(touched, new_coef_hbm.at[place, :], sems.at[4])]
    ends[0].start()
    for at, strip in enumerate(strips):
        change_residuals(0, strip)
        ends.append(
            pltpu.make_async_copy(residual_ref.at[strip, :], new_residual_hbm.at[strip, :], sems.at[5 + at])
        )
        ends[-1].start()
    for copy in ends:
        copy.wait()


def solve(core, own, other, total, kernel, residuals, coefficients, place, mine):
    rows, size = kernel.shape
    outs = residuals.shape[1]
    vmem, smem = pl.BlockSpec(memory_space=pltpu.VMEM), pl.BlockSpec(memory_space=pltpu.SMEM)
    away = pl.BlockSpec(memory_space=pltpu.HBM)
    return pl.pallas_call(
        functools.partial(solve_kernel, total),
        out_shape=[jax.ShapeDtypeStruct((rows, outs), f32)] * 2,
        in_specs=[smem] * 3 + [vmem] * 6 + [away] * 3,
        out_specs=[away] * 2,
        scratch_shapes=[
            pltpu.VMEM((size, size + outs), f32),
            pltpu.VMEM((TILE, TILE), f32),
            pltpu.VMEM((size // TILE, TILE, TILE), f32),
            pltpu.VMEM((size, outs), f32),
            pltpu.VMEM((rows, size), bf16),
            pltpu.VMEM((rows, outs), f32),
            pltpu.VMEM((rows, outs), f32),
            pltpu.VMEM((size, outs), f32),
            pltpu.SemaphoreType.DMA((5 + rows // STRIP,)),
        ],
        compiler_params=pltpu.CompilerParams(vmem_limit_bytes=50 << 20),
    )(
        core.reshape(1),
        place.astype(jnp.int32).reshape(1),
        mine.astype(jnp.int32).reshape(1),
        *own,
        *other,
        kernel,
        residuals,
        coefficients,
    )


def body(examples, residuals, coefficients, block_index):
    rows_here = examples.shape[0]
    features = examples.shape[1]
    outs = residuals.shape[1]
    per_device = rows_here // BLOCK
    total_examples = rows_here * lax.axis_size(AXES)
    chosen = block_index[0]
    owner_rank = chosen // per_device
    offset = chosen % per_device * BLOCK
    is_owner = owner_rank == lax.axis_index(AXES)
    core_pick = rank_bits()[0], rank_bits()[0]
    core = is_high(core_pick)
    first_width = features * 5 // 8 // TILE * TILE

    whole = jnp.where(is_owner, lax.dynamic_slice_in_dim(examples, offset, BLOCK, 0), 0).astype(examples.dtype)

    def masked(half):
        return lax.dynamic_slice_in_dim(whole, half * (BLOCK // 2), BLOCK // 2, 0)

    sq_rows = jnp.sum(jnp.square(examples.astype(f32)), axis=1)
    low = residuals.astype(bf16)
    cuts = ((0, first_width), (first_width, features))
    (own,), (other,), (sq_rows, low, coefficients) = sum_parts(
        [masked(1 - core)], [masked(core)], 1, cuts, (sq_rows, low, coefficients)
    )
    block_rows = in_order(own, other, core_pick)
    sq_block = jnp.sum(jnp.square(block_rows.astype(f32)), axis=1)
    inner = lax.dot_general(examples, block_rows, (((1,), (1,)), ((), ())), preferred_element_type=f32)
    kernel = jnp.exp(
        -width_factor * (sq_rows[:, None] + sq_block[None, :] - 2.0 * inner) / features
    ).astype(bf16)
    own_coef = lax.dynamic_slice_in_dim(coefficients, offset, BLOCK, 0)
    weight_own = jnp.where(is_owner, total_examples * ridge, 0.0).astype(f32)
    keep, give = products(core, kernel, low, own_coef, weight_own)
    own, other, _ = sum_parts(give, keep, 0)
    place = chosen % per_device
    return tuple(solve(core, own, other, total_examples, kernel, residuals, coefficients, place, is_owner))


def solution(mesh):
    in_specs = (P(("row", "col"), None), P(("row", "col"), None), P(("row", "col"), None), P())
    out_specs = (P(("row", "col"), None), P(("row", "col"), None))
    return jax.shard_map(body, mesh=mesh, in_specs=in_specs, out_specs=out_specs, check_vma=False)
```

```python
import functools

import jax
import jax.numpy as jnp
from jax import lax
from jax.experimental import pallas as pl
from jax.experimental.pallas import tpu as pltpu
from jax.sharding import PartitionSpec as P

BLOCK = 1024
TILE = 128
SUB = 8
STRIP = 512
AXES = ("row", "col")

ridge = 0.001
width_factor = 0.5
f32 = jnp.float32
bf16 = jnp.bfloat16


def rank_bits():
    def masks(size, unit):
        found = []
        while size > 1:
            found.append(unit)
            unit, size = unit * 2, size // 2
        return found
    columns = lax.axis_size("col")
    col, row = masks(columns, 1), masks(lax.axis_size("row"), columns)
    return col[0], (col[1], col[2], row[0]), col[3:] + row[1:]


def swap(value, pick):
    size = lax.axis_size(AXES)
    return lax.ppermute(value, AXES, [(i, i ^ pick[i % 2]) for i in range(size)])


def is_high(pick):
    rank = lax.axis_index(AXES)
    mask = jnp.where(rank % 2 == 0, pick[0], pick[1])
    return (rank // mask) % 2


def halve(value, pick):
    rows = value.shape[0] // 2
    high = is_high(pick)
    keep = lax.dynamic_slice_in_dim(value, high * rows, rows, 0)
    give = lax.dynamic_slice_in_dim(value, (1 - high) * rows, rows, 0)
    return keep + swap(give, pick)


def in_order(value, other, pick):
    low = is_high(pick) == 0
    return jnp.concatenate([jnp.where(low, value, other), jnp.where(low, other, value)], axis=0)


def sum_parts(give, keep, axis, cuts=(), beside=()):
    core, (x, y, z), far = rank_bits()
    both = (core, core)
    if cuts:
        orders = [[(x, y), (y, z), (z, x)], [(z, z), (x, x), (y, y)]]
    else:
        orders = [[(x, x), (y, y), (z, z)], [(y, y), (z, z), (x, x)], [(z, z), (x, x), (y, y)]]
    if cuts:
        whole = keep[0] + swap(give[0], both)
        parts = [lax.slice_in_dim(whole, low, high, axis=axis) for low, high in cuts]
    else:
        moved = [swap(part, both) for part in give]
        parts = [part + other for part, other in zip(keep, moved)]
    for step in range(3):
        parts = [halve(part, order[step]) for part, order in zip(parts, orders)]
        if step == 0 and beside:
            parts, beside = lax.optimization_barrier((parts, beside))
    if cuts:
        sizes = [part.shape[axis] for part in parts]
        whole = jnp.concatenate(parts, axis=axis)
        for mask in far:
            whole = whole + swap(whole, (mask, mask))
        parts = [
            lax.slice_in_dim(whole, 0, sizes[0], axis=axis),
            lax.slice_in_dim(whole, sizes[0], sum(sizes), axis=axis),
        ]
    else:
        for mask in far:
            parts = [part + swap(part, (mask, mask)) for part in parts]
    for step in (2, 1, 0):
        parts = [in_order(part, swap(part, order[step]), order[step]) for part, order in zip(parts, orders)]
    if cuts:
        parts = [jnp.concatenate(parts, axis=axis)]
    return parts, [swap(part, both) for part in parts], beside


def half_tiles(blocks, outs, half):
    split = blocks // 2
    rows = range(split) if half == 0 else range(split, blocks)
    tiles = [(row, col) for row in rows for col in range(row, blocks)]
    if half:
        tiles += [(row, blocks + b) for row in range(blocks) for b in range(outs // TILE)]
    return tiles


def part_sizes(blocks, outs):
    tiles = len(half_tiles(blocks, outs, 0))
    assert tiles == len(half_tiles(blocks, outs, 1))
    return [(tiles + 2 - i) // 3 for i in range(3)]


def part_place(sizes, index):
    for part, size in enumerate(sizes):
        if index < size:
            return part, slice(index * TILE, (index + 1) * TILE)
        index -= size


def products_kernel(sizes, core_ref, kernel_ref, low_ref, coef_ref, weight_ref, *refs):
    keep_refs, give_refs, packed = refs[:3], refs[3:6], refs[6]
    size, outs = kernel_ref.shape[1], low_ref.shape[1]
    blocks = size // TILE
    step = 2 * TILE
    contract = (((0,), (0,)), ((), ()))
    tiles = half_tiles(blocks, outs, 0) + half_tiles(blocks, outs, 1)
    place = {tile: slice(index * TILE, (index + 1) * TILE) for index, tile in enumerate(tiles)}

    def put(value, row, col):
        for a in range(value.shape[0] // TILE):
            for b in range(value.shape[1] // TILE):
                if (row + a, col + b) in place:
                    packed[place[row + a, col + b], :] = value[a * TILE : (a + 1) * TILE, b * TILE : (b + 1) * TILE]

    for i in range(size // step):
        left = kernel_ref[:, i * step : (i + 1) * step]
        put(lax.dot_general(left, kernel_ref[:, i * step :], contract, preferred_element_type=f32), 2 * i, 2 * i)
        grad = lax.dot_general(left, low_ref[...], contract, preferred_element_type=f32)
        put(grad - weight_ref[0] * coef_ref[i * step : (i + 1) * step, :], 2 * i, blocks)
    first = core_ref[0] == 0
    start, half = 0, sum(sizes) * TILE
    for part, count in enumerate(sizes):
        rows = count * TILE
        low, high = packed[start : start + rows, :], packed[half + start : half + start + rows, :]
        keep_refs[part][...] = jnp.where(first, low, high)
        give_refs[part][...] = jnp.where(first, high, low)
        start += rows


def products(core, kernel, low, own_coef, weight):
    size, outs = kernel.shape[1], low.shape[1]
    sizes = part_sizes(size // TILE, outs)
    vmem = pl.BlockSpec(memory_space=pltpu.VMEM)
    smem = pl.BlockSpec(memory_space=pltpu.SMEM)
    found = pl.pallas_call(
        functools.partial(products_kernel, sizes),
        out_shape=[jax.ShapeDtypeStruct((count * TILE, TILE), f32) for count in sizes] * 2,
        in_specs=[smem, vmem, vmem, vmem, smem],
        out_specs=[vmem] * 6,
        scratch_shapes=[pltpu.VMEM((2 * sum(sizes) * TILE, TILE), f32)],
        compiler_params=pltpu.CompilerParams(vmem_limit_bytes=24 << 20),
    )(core.reshape(1), kernel, low, own_coef, weight.reshape(1))
    return found[:3], found[3:]


def split_three(value):
    high = value.astype(bf16).astype(f32)
    rest = value - high
    middle = rest.astype(bf16).astype(f32)
    return high, middle, rest - middle


def left_six(value, axis):
    h, m, l = split_three(value)
    return jnp.concatenate([h, h, m, h, l, m], axis=axis).astype(bf16)


def right_six(value):
    h, m, l = split_three(value)
    return jnp.concatenate([h, m, h, l, h, m], axis=0).astype(bf16)


def dot6(left, right):
    return lax.dot_general(left, right, (((1,), (0,)), ((), ())), preferred_element_type=f32)


def down(value, row):
    return jnp.broadcast_to(value[row : row + 1, :], (SUB, TILE))


def across(value, lane):
    return jnp.broadcast_to(value[:, lane : lane + 1], (SUB, TILE))


def factor_block(pair, inverse_ref):
    steps = TILE // SUB
    place = lax.broadcasted_iota(jnp.int32, (SUB, TILE), 0)
    lane = lax.broadcasted_iota(jnp.int32, (SUB, TILE), 1)
    lanes = lax.broadcasted_iota(jnp.int32, (TILE, TILE), 1)
    rows = pair[0:SUB, :]
    near = pair[SUB : 2 * SUB, :]
    corner = [across(rows, c) for c in range(SUB)]
    for j in range(steps):
        at = j * SUB
        inside = (lane >= at) & (lane < at + SUB)
        block = corner
        rows = jnp.where(inside, jnp.where(lane - at == place, 1.0, 0.0), rows)
        flat = [down(rows, i) for i in range(SUB)]
        lower = []
        if j + 1 < steps:
            lower.append(near)
            corner = [across(near, at + SUB + c) for c in range(SUB)]
        if j + 2 < steps:
            lower.append(pair[at + 2 * SUB : at + 3 * SUB, :])
        tall = [[across(group, at + i) for i in range(SUB)] for group in lower]
        lower = [jnp.where(inside, 0.0, group) for group in lower]
        for p in range(SUB):
            root = lax.rsqrt(down(block[p], p))
            column = block[p] * root
            upper = {k: down(column, k) for k in range(p + 1, SUB)}
            block = [value - column * upper[c] if c > p else value for c, value in enumerate(block)]
            flat[p] = flat[p] * root
            for group in tall:
                group[p] = group[p] * root
            for k in range(p + 1, SUB):
                flat[k] = flat[k] - upper[k] * flat[p]
                for group in tall:
                    group[k] = group[k] - upper[k] * group[p]
            if lower:
                corner = [corner[c] - tall[0][p] * down(tall[0][p], c) for c in range(SUB)]
            lower = [group - high[p] * flat[p] for group, high in zip(lower, tall)]
        found = flat[SUB - 1]
        for i in range(SUB - 1):
            found = jnp.where(place == i, flat[i], found)
        inverse_ref[at : at + SUB, :] = jnp.where(lane < at + SUB, found, 0.0)
        if j + 3 < steps:
            h, m, l = split_three(found)
            left = jnp.concatenate([h, h, m, h, l, m], axis=0).astype(bf16)
            right = jnp.concatenate([h, m, h, l, h, m], axis=0).astype(bf16)
            change = lax.dot_general(left, right, (((0,), (0,)), ((), ())), preferred_element_type=f32)
            below = slice(at + 3 * SUB, TILE)
            here = lanes[below]
            pair[below, :] = jnp.where((here >= at) & (here < at + SUB), 0.0, pair[below, :]) - change[below]
        if lower:
            rows = lower[0]
        if len(lower) > 1:
            near = lower[1]


def solve_kernel(total, core_ref, place_ref, mine_ref, *refs):
    own_refs, other_refs, (kernel_hbm, residual_hbm, coef_hbm) = refs[:3], refs[3:6], refs[6:9]
    new_residual_hbm, new_coef_hbm, system, pair, inverses, update = refs[9:15]
    kernel_ref, residual_ref, coef_ref, touched, sems = refs[15:]
    copies = [
        pltpu.make_async_copy(source, target, sems.at[at])
        for at, (source, target) in enumerate(
            ((kernel_hbm, kernel_ref), (residual_hbm, residual_ref), (coef_hbm, coef_ref), (coef_ref, new_coef_hbm))
        )
    ]
    for copy in copies[:3]:
        copy.start()
    size, outs = update.shape
    width = size + outs
    blocks = size // TILE
    scale = 1.0 / total
    sizes = part_sizes(blocks, outs)
    for half in range(2):
        mine = core_ref[0] == half
        for index, (row, col) in enumerate(half_tiles(blocks, outs, half)):
            part, rows = part_place(sizes, index)
            value = jnp.where(mine, own_refs[part][rows, :], other_refs[part][rows, :])
            system[row * TILE : (row + 1) * TILE, col * TILE : (col + 1) * TILE] = value * scale
    unit = jnp.where(
        lax.broadcasted_iota(jnp.int32, (TILE, TILE), 0) == lax.broadcasted_iota(jnp.int32, (TILE, TILE), 1), 1.0, 0.0
    ).astype(f32)

    def forward(k, _):
        @pl.when(k == blocks // 2)
        def _():
            copies[2].wait()
            copies[3].start()

        here = pl.ds(pl.multiple_of(k * TILE, TILE), TILE)
        pair[...] = system[here, here] + ridge * unit
        factor_block(pair, inverses.at[k])
        for kk in range(blocks):

            @pl.when(k == kk)
            def _(kk=kk):
                first = (kk + 1) * TILE
                mine = slice(kk * TILE, first)
                inverse = inverses[kk]
                found = dot6(left_six(inverse, 1), right_six(system[mine, first:]))
                right = right_six(found)
                system[mine, first:] = dot6(left_six(inverse.T, 1), right)
                if kk + 1 < blocks:
                    left = left_six(found[:, : size - first].T, 1)
                    for at in range(first, size, 2 * TILE):
                        end = min(at + 2 * TILE, size)
                        system[at:end, at:] = system[at:end, at:] - dot6(left[at - first : end - first], right[:, at - first :])
        return 0

    lax.fori_loop(0, blocks, forward, 0)
    copies[3].wait()
    copies[0].wait()
    copies[1].wait()

    def change_residuals(k, strip):
        lanes = slice(k * TILE, (k + 2) * TILE)
        low = update[lanes, :].astype(bf16)
        change = jnp.dot(kernel_ref[strip, lanes], low, preferred_element_type=f32)
        residual_ref[strip, :] = residual_ref[strip, :] - change

    strips = [slice(at, at + STRIP) for at in range(0, residual_ref.shape[0], STRIP)]
    for k in reversed(range(blocks)):
        mine = slice(k * TILE, (k + 1) * TILE)
        found = system[mine, size:]
        update[mine, :] = found
        if k:
            left = left_six(system[: k * TILE, mine], 1)
            system[: k * TILE, size:] = system[: k * TILE, size:] - dot6(left, right_six(found))
        if k and k % 2 == 0:
            for strip in strips:
                change_residuals(k, strip)
    place = pl.ds(pl.multiple_of(place_ref[0] * size, size), size)
    chosen = coef_ref[place, :]
    touched[...] = jnp.where(mine_ref[0] == 1, chosen + update[...], chosen)
    ends = [pltpu.make_async_copy(touched, new_coef_hbm.at[place, :], sems.at[4])]
    ends[0].start()
    for at, strip in enumerate(strips):
        change_residuals(0, strip)
        ends.append(
            pltpu.make_async_copy(residual_ref.at[strip, :], new_residual_hbm.at[strip, :], sems.at[5 + at])
        )
        ends[-1].start()
    for copy in ends:
        copy.wait()


def solve(core, own, other, total, kernel, residuals, coefficients, place, mine):
    rows, size = kernel.shape
    outs = residuals.shape[1]
    vmem, smem = pl.BlockSpec(memory_space=pltpu.VMEM), pl.BlockSpec(memory_space=pltpu.SMEM)
    away = pl.BlockSpec(memory_space=pltpu.HBM)
    return pl.pallas_call(
        functools.partial(solve_kernel, total),
        out_shape=[jax.ShapeDtypeStruct((rows, outs), f32)] * 2,
        in_specs=[smem] * 3 + [vmem] * 6 + [away] * 3,
        out_specs=[away] * 2,
        scratch_shapes=[
            pltpu.VMEM((size, size + outs), f32),
            pltpu.VMEM((TILE, TILE), f32),
            pltpu.VMEM((size // TILE, TILE, TILE), f32),
            pltpu.VMEM((size, outs), f32),
            pltpu.VMEM((rows, size), bf16),
            pltpu.VMEM((rows, outs), f32),
            pltpu.VMEM((rows, outs), f32),
            pltpu.VMEM((size, outs), f32),
            pltpu.SemaphoreType.DMA((5 + rows // STRIP,)),
        ],
        compiler_params=pltpu.CompilerParams(vmem_limit_bytes=50 << 20),
    )(
        core.reshape(1),
        place.astype(jnp.int32).reshape(1),
        mine.astype(jnp.int32).reshape(1),
        *own,
        *other,
        kernel,
        residuals,
        coefficients,
    )


def body(examples, residuals, coefficients, block_index):
    rows_here = examples.shape[0]
    features = examples.shape[1]
    outs = residuals.shape[1]
    per_device = rows_here // BLOCK
    total_examples = rows_here * lax.axis_size(AXES)
    chosen = block_index[0]
    owner_rank = chosen // per_device
    offset = chosen % per_device * BLOCK
    is_owner = owner_rank == lax.axis_index(AXES)
    core_pick = rank_bits()[0], rank_bits()[0]
    core = is_high(core_pick)
    first_width = features * 5 // 8 // TILE * TILE

    whole = jnp.where(is_owner, lax.dynamic_slice_in_dim(examples, offset, BLOCK, 0), 0).astype(examples.dtype)

    def masked(half):
        return lax.dynamic_slice_in_dim(whole, half * (BLOCK // 2), BLOCK // 2, 0)

    sq_rows = jnp.sum(jnp.square(examples.astype(f32)), axis=1)
    low = residuals.astype(bf16)
    cuts = ((0, first_width), (first_width, features))
    (own,), (other,), (sq_rows, low, coefficients) = sum_parts(
        [masked(1 - core)], [masked(core)], 1, cuts, (sq_rows, low, coefficients)
    )
    block_rows = in_order(own, other, core_pick)
    sq_block = jnp.sum(jnp.square(block_rows.astype(f32)), axis=1)
    inner = lax.dot_general(examples, block_rows, (((1,), (1,)), ((), ())), preferred_element_type=f32)
    kernel = jnp.exp(
        -width_factor * (sq_rows[:, None] + sq_block[None, :] - 2.0 * inner) / features
    ).astype(bf16)
    own_coef = lax.dynamic_slice_in_dim(coefficients, offset, BLOCK, 0)
    weight_own = jnp.where(is_owner, total_examples * ridge, 0.0).astype(f32)
    keep, give = products(core, kernel, low, own_coef, weight_own)
    own, other, _ = sum_parts(give, keep, 0)
    place = chosen % per_device
    return tuple(solve(core, own, other, total_examples, kernel, residuals, coefficients, place, is_owner))


def solution(mesh):
    in_specs = (P(("row", "col"), None), P(("row", "col"), None), P(("row", "col"), None), P())
    out_specs = (P(("row", "col"), None), P(("row", "col"), None))
    return jax.shard_map(body, mesh=mesh, in_specs=in_specs, out_specs=out_specs, check_vma=False)
```

```python
import functools

import jax
import jax.numpy as jnp
from jax import lax
from jax.experimental import pallas as pl
from jax.experimental.pallas import tpu as pltpu
from jax.sharding import PartitionSpec as P

BLOCK = 1024
TILE = 128
SUB = 8
STRIP = 512
AXES = ("row", "col")

ridge = 0.001
width_factor = 0.5
f32 = jnp.float32
bf16 = jnp.bfloat16


def rank_bits():
    def masks(size, unit):
        found = []
        while size > 1:
            found.append(unit)
            unit, size = unit * 2, size // 2
        return found
    columns = lax.axis_size("col")
    col, row = masks(columns, 1), masks(lax.axis_size("row"), columns)
    return col[0], (col[1], col[2], row[0]), col[3:] + row[1:]


def swap(value, pick):
    size = lax.axis_size(AXES)
    return lax.ppermute(value, AXES, [(i, i ^ pick[i % 2]) for i in range(size)])


def is_high(pick):
    rank = lax.axis_index(AXES)
    mask = jnp.where(rank % 2 == 0, pick[0], pick[1])
    return (rank // mask) % 2


def halve(value, pick):
    rows = value.shape[0] // 2
    high = is_high(pick)
    keep = lax.dynamic_slice_in_dim(value, high * rows, rows, 0)
    give = lax.dynamic_slice_in_dim(value, (1 - high) * rows, rows, 0)
    return keep + swap(give, pick)


def in_order(value, other, pick):
    low = is_high(pick) == 0
    return jnp.concatenate([jnp.where(low, value, other), jnp.where(low, other, value)], axis=0)


def sum_parts(give, keep, axis, cuts=(), beside=()):
    core, (x, y, z), far = rank_bits()
    both = (core, core)
    if cuts:
        orders = [[(x, y), (y, z), (z, x)], [(z, z), (x, x), (y, y)]]
    else:
        orders = [[(x, x), (y, y), (z, z)], [(y, y), (z, z), (x, x)], [(z, z), (x, x), (y, y)]]
    if cuts:
        whole = keep[0] + swap(give[0], both)
        parts = [lax.slice_in_dim(whole, low, high, axis=axis) for low, high in cuts]
    else:
        moved = [swap(part, both) for part in give]
        parts = [part + other for part, other in zip(keep, moved)]
    for step in range(3):
        parts = [halve(part, order[step]) for part, order in zip(parts, orders)]
        if step == 0 and beside:
            parts, beside = lax.optimization_barrier((parts, beside))
    if cuts:
        sizes = [part.shape[axis] for part in parts]
        whole = jnp.concatenate(parts, axis=axis)
        for mask in far:
            whole = whole + swap(whole, (mask, mask))
        parts = [
            lax.slice_in_dim(whole, 0, sizes[0], axis=axis),
            lax.slice_in_dim(whole, sizes[0], sum(sizes), axis=axis),
        ]
    else:
        for mask in far:
            parts = [part + swap(part, (mask, mask)) for part in parts]
    for step in (2, 1, 0):
        parts = [in_order(part, swap(part, order[step]), order[step]) for part, order in zip(parts, orders)]
    if cuts:
        parts = [jnp.concatenate(parts, axis=axis)]
    return parts, [swap(part, both) for part in parts], beside


def half_tiles(blocks, outs, half):
    split = blocks // 2
    rows = range(split) if half == 0 else range(split, blocks)
    tiles = [(row, col) for row in rows for col in range(row, blocks)]
    if half:
        tiles += [(row, blocks + b) for row in range(blocks) for b in range(outs // TILE)]
    return tiles


def part_sizes(blocks, outs):
    tiles = len(half_tiles(blocks, outs, 0))
    assert tiles == len(half_tiles(blocks, outs, 1))
    return [(tiles + 2 - i) // 3 for i in range(3)]


def part_place(sizes, index):
    for part, size in enumerate(sizes):
        if index < size:
            return part, slice(index * TILE, (index + 1) * TILE)
        index -= size


def products_kernel(sizes, core_ref, kernel_ref, low_ref, coef_ref, weight_ref, *refs):
    keep_refs, give_refs, packed = refs[:3], refs[3:6], refs[6]
    size, outs = kernel_ref.shape[1], low_ref.shape[1]
    blocks = size // TILE
    step = 2 * TILE
    contract = (((0,), (0,)), ((), ()))
    tiles = half_tiles(blocks, outs, 0) + half_tiles(blocks, outs, 1)
    place = {tile: slice(index * TILE, (index + 1) * TILE) for index, tile in enumerate(tiles)}

    def put(value, row, col):
        for a in range(value.shape[0] // TILE):
            for b in range(value.shape[1] // TILE):
                if (row + a, col + b) in place:
                    packed[place[row + a, col + b], :] = value[a * TILE : (a + 1) * TILE, b * TILE : (b + 1) * TILE]

    for i in range(size // step):
        left = kernel_ref[:, i * step : (i + 1) * step]
        put(lax.dot_general(left, kernel_ref[:, i * step :], contract, preferred_element_type=f32), 2 * i, 2 * i)
    grad = lax.dot_general(kernel_ref[...], low_ref[...], contract, preferred_element_type=f32)
    put(grad - weight_ref[0] * coef_ref[...], 0, blocks)
    first = core_ref[0] == 0
    start, half = 0, sum(sizes) * TILE
    for part, count in enumerate(sizes):
        rows = count * TILE
        low, high = packed[start : start + rows, :], packed[half + start : half + start + rows, :]
        keep_refs[part][...] = jnp.where(first, low, high)
        give_refs[part][...] = jnp.where(first, high, low)
        start += rows


def products(core, kernel, low, own_coef, weight):
    size, outs = kernel.shape[1], low.shape[1]
    sizes = part_sizes(size // TILE, outs)
    vmem = pl.BlockSpec(memory_space=pltpu.VMEM)
    smem = pl.BlockSpec(memory_space=pltpu.SMEM)
    found = pl.pallas_call(
        functools.partial(products_kernel, sizes),
        out_shape=[jax.ShapeDtypeStruct((count * TILE, TILE), f32) for count in sizes] * 2,
        in_specs=[smem, vmem, vmem, vmem, smem],
        out_specs=[vmem] * 6,
        scratch_shapes=[pltpu.VMEM((2 * sum(sizes) * TILE, TILE), f32)],
        compiler_params=pltpu.CompilerParams(vmem_limit_bytes=24 << 20),
    )(core.reshape(1), kernel, low, own_coef, weight.reshape(1))
    return found[:3], found[3:]


def split_three(value):
    high = value.astype(bf16).astype(f32)
    rest = value - high
    middle = rest.astype(bf16).astype(f32)
    return high, middle, rest - middle


def left_six(value, axis):
    h, m, l = split_three(value)
    return jnp.concatenate([h, h, m, h, l, m], axis=axis).astype(bf16)


def right_six(value):
    h, m, l = split_three(value)
    return jnp.concatenate([h, m, h, l, h, m], axis=0).astype(bf16)


def dot6(left, right):
    return lax.dot_general(left, right, (((1,), (0,)), ((), ())), preferred_element_type=f32)


def down(value, row):
    return jnp.broadcast_to(value[row : row + 1, :], (SUB, TILE))


def across(value, lane):
    return jnp.broadcast_to(value[:, lane : lane + 1], (SUB, TILE))


def factor_block(pair, inverse_ref):
    steps = TILE // SUB
    place = lax.broadcasted_iota(jnp.int32, (SUB, TILE), 0)
    lane = lax.broadcasted_iota(jnp.int32, (SUB, TILE), 1)
    lanes = lax.broadcasted_iota(jnp.int32, (TILE, TILE), 1)
    rows = pair[0:SUB, :]
    near = pair[SUB : 2 * SUB, :]
    corner = [across(rows, c) for c in range(SUB)]
    for j in range(steps):
        at = j * SUB
        inside = (lane >= at) & (lane < at + SUB)
        block = corner
        rows = jnp.where(inside, jnp.where(lane - at == place, 1.0, 0.0), rows)
        flat = [down(rows, i) for i in range(SUB)]
        lower = []
        if j + 1 < steps:
            lower.append(near)
            corner = [across(near, at + SUB + c) for c in range(SUB)]
        if j + 2 < steps:
            lower.append(pair[at + 2 * SUB : at + 3 * SUB, :])
        tall = [[across(group, at + i) for i in range(SUB)] for group in lower]
        lower = [jnp.where(inside, 0.0, group) for group in lower]
        for p in range(SUB):
            root = lax.rsqrt(down(block[p], p))
            column = block[p] * root
            upper = {k: down(column, k) for k in range(p + 1, SUB)}
            block = [value - column * upper[c] if c > p else value for c, value in enumerate(block)]
            flat[p] = flat[p] * root
            for group in tall:
                group[p] = group[p] * root
            for k in range(p + 1, SUB):
                flat[k] = flat[k] - upper[k] * flat[p]
                for group in tall:
                    group[k] = group[k] - upper[k] * group[p]
            if lower:
                corner = [corner[c] - tall[0][p] * down(tall[0][p], c) for c in range(SUB)]
            lower = [group - high[p] * flat[p] for group, high in zip(lower, tall)]
        found = flat[SUB - 1]
        for i in range(SUB - 1):
            found = jnp.where(place == i, flat[i], found)
        inverse_ref[at : at + SUB, :] = jnp.where(lane < at + SUB, found, 0.0)
        if j + 3 < steps:
            h, m, l = split_three(found)
            left = jnp.concatenate([h, h, m, h, l, m], axis=0).astype(bf16)
            right = jnp.concatenate([h, m, h, l, h, m], axis=0).astype(bf16)
            change = lax.dot_general(left, right, (((0,), (0,)), ((), ())), preferred_element_type=f32)
            below = slice(at + 3 * SUB, TILE)
            here = lanes[below]
            pair[below, :] = jnp.where((here >= at) & (here < at + SUB), 0.0, pair[below, :]) - change[below]
        if lower:
            rows = lower[0]
        if len(lower) > 1:
            near = lower[1]


def solve_kernel(total, core_ref, place_ref, mine_ref, *refs):
    own_refs, other_refs, (kernel_hbm, residual_hbm, coef_hbm) = refs[:3], refs[3:6], refs[6:9]
    new_residual_hbm, new_coef_hbm, system, pair, inverses, update = refs[9:15]
    kernel_ref, residual_ref, coef_ref, touched, sems = refs[15:]
    copies = [
        pltpu.make_async_copy(source, target, sems.at[at])
        for at, (source, target) in enumerate(
            ((kernel_hbm, kernel_ref), (residual_hbm, residual_ref), (coef_hbm, coef_ref), (coef_ref, new_coef_hbm))
        )
    ]
    for copy in copies[:3]:
        copy.start()
    size, outs = update.shape
    width = size + outs
    blocks = size // TILE
    scale = 1.0 / total
    sizes = part_sizes(blocks, outs)
    for half in range(2):
        mine = core_ref[0] == half
        for index, (row, col) in enumerate(half_tiles(blocks, outs, half)):
            part, rows = part_place(sizes, index)
            value = jnp.where(mine, own_refs[part][rows, :], other_refs[part][rows, :])
            system[row * TILE : (row + 1) * TILE, col * TILE : (col + 1) * TILE] = value * scale
    unit = jnp.where(
        lax.broadcasted_iota(jnp.int32, (TILE, TILE), 0) == lax.broadcasted_iota(jnp.int32, (TILE, TILE), 1), 1.0, 0.0
    ).astype(f32)

    def forward(k, _):
        @pl.when(k == blocks // 2)
        def _():
            copies[2].wait()
            copies[3].start()

        here = pl.ds(pl.multiple_of(k * TILE, TILE), TILE)
        pair[...] = system[here, here] + ridge * unit
        factor_block(pair, inverses.at[k])
        for kk in range(blocks):

            @pl.when(k == kk)
            def _(kk=kk):
                first = (kk + 1) * TILE
                mine = slice(kk * TILE, first)
                inverse = inverses[kk]
                found = dot6(left_six(inverse, 1), right_six(system[mine, first:]))
                right = right_six(found)
                system[mine, first:] = dot6(left_six(inverse.T, 1), right)
                if kk + 1 < blocks:
                    left = left_six(found[:, : size - first].T, 1)
                    for at in range(first, size, 2 * TILE):
                        end = min(at + 2 * TILE, size)
                        system[at:end, at:] = system[at:end, at:] - dot6(left[at - first : end - first], right[:, at - first :])
        return 0

    lax.fori_loop(0, blocks, forward, 0)
    copies[3].wait()
    copies[0].wait()
    copies[1].wait()

    def change_residuals(k, strip):
        lanes = slice(k * TILE, (k + 2) * TILE)
        low = update[lanes, :].astype(bf16)
        change = jnp.dot(kernel_ref[strip, lanes], low, preferred_element_type=f32)
        residual_ref[strip, :] = residual_ref[strip, :] - change

    strips = [slice(at, at + STRIP) for at in range(0, residual_ref.shape[0], STRIP)]
    for k in reversed(range(blocks)):
        mine = slice(k * TILE, (k + 1) * TILE)
        found = system[mine, size:]
        update[mine, :] = found
        if k:
            left = left_six(system[: k * TILE, mine], 1)
            system[: k * TILE, size:] = system[: k * TILE, size:] - dot6(left, right_six(found))
        if k and k % 2 == 0:
            for strip in strips:
                change_residuals(k, strip)
    place = pl.ds(pl.multiple_of(place_ref[0] * size, size), size)
    chosen = coef_ref[place, :]
    touched[...] = jnp.where(mine_ref[0] == 1, chosen + update[...], chosen)
    ends = [pltpu.make_async_copy(touched, new_coef_hbm.at[place, :], sems.at[4])]
    ends[0].start()
    for at, strip in enumerate(strips):
        change_residuals(0, strip)
        ends.append(
            pltpu.make_async_copy(residual_ref.at[strip, :], new_residual_hbm.at[strip, :], sems.at[5 + at])
        )
        ends[-1].start()
    for copy in ends:
        copy.wait()


def solve(core, own, other, total, kernel, residuals, coefficients, place, mine):
    rows, size = kernel.shape
    outs = residuals.shape[1]
    vmem, smem = pl.BlockSpec(memory_space=pltpu.VMEM), pl.BlockSpec(memory_space=pltpu.SMEM)
    away = pl.BlockSpec(memory_space=pltpu.HBM)
    return pl.pallas_call(
        functools.partial(solve_kernel, total),
        out_shape=[jax.ShapeDtypeStruct((rows, outs), f32)] * 2,
        in_specs=[smem] * 3 + [vmem] * 6 + [away] * 3,
        out_specs=[away] * 2,
        scratch_shapes=[
            pltpu.VMEM((size, size + outs), f32),
            pltpu.VMEM((TILE, TILE), f32),
            pltpu.VMEM((size // TILE, TILE, TILE), f32),
            pltpu.VMEM((size, outs), f32),
            pltpu.VMEM((rows, size), bf16),
            pltpu.VMEM((rows, outs), f32),
            pltpu.VMEM((rows, outs), f32),
            pltpu.VMEM((size, outs), f32),
            pltpu.SemaphoreType.DMA((5 + rows // STRIP,)),
        ],
        compiler_params=pltpu.CompilerParams(vmem_limit_bytes=50 << 20),
    )(
        core.reshape(1),
        place.astype(jnp.int32).reshape(1),
        mine.astype(jnp.int32).reshape(1),
        *own,
        *other,
        kernel,
        residuals,
        coefficients,
    )


def body(examples, residuals, coefficients, block_index):
    rows_here = examples.shape[0]
    features = examples.shape[1]
    outs = residuals.shape[1]
    per_device = rows_here // BLOCK
    total_examples = rows_here * lax.axis_size(AXES)
    chosen = block_index[0]
    owner_rank = chosen // per_device
    offset = chosen % per_device * BLOCK
    is_owner = owner_rank == lax.axis_index(AXES)
    core_pick = rank_bits()[0], rank_bits()[0]
    core = is_high(core_pick)
    first_width = features * 5 // 8 // TILE * TILE

    whole = jnp.where(is_owner, lax.dynamic_slice_in_dim(examples, offset, BLOCK, 0), 0).astype(examples.dtype)

    def masked(half):
        return lax.dynamic_slice_in_dim(whole, half * (BLOCK // 2), BLOCK // 2, 0)

    sq_rows = jnp.sum(jnp.square(examples.astype(f32)), axis=1)
    low = residuals.astype(bf16)
    cuts = ((0, first_width), (first_width, features))
    (own,), (other,), (sq_rows, low, coefficients) = sum_parts(
        [masked(1 - core)], [masked(core)], 1, cuts, (sq_rows, low, coefficients)
    )
    block_rows = in_order(own, other, core_pick)
    sq_block = jnp.sum(jnp.square(block_rows.astype(f32)), axis=1)
    inner = lax.dot_general(examples, block_rows, (((1,), (1,)), ((), ())), preferred_element_type=f32)
    kernel = jnp.exp(
        -width_factor * (sq_rows[:, None] + sq_block[None, :] - 2.0 * inner) / features
    ).astype(bf16)
    own_coef = lax.dynamic_slice_in_dim(coefficients, offset, BLOCK, 0)
    weight_own = jnp.where(is_owner, total_examples * ridge, 0.0).astype(f32)
    keep, give = products(core, kernel, low, own_coef, weight_own)
    own, other, _ = sum_parts(give, keep, 0)
    place = chosen % per_device
    return tuple(solve(core, own, other, total_examples, kernel, residuals, coefficients, place, is_owner))


def solution(mesh):
    in_specs = (P(("row", "col"), None), P(("row", "col"), None), P(("row", "col"), None), P())
    out_specs = (P(("row", "col"), None), P(("row", "col"), None))
    return jax.shard_map(body, mesh=mesh, in_specs=in_specs, out_specs=out_specs, check_vma=False)
```
